512 devices in a mesh: al: 16 (over z_lo, x), row: 32 (over y, z_hi, core).
Axes of the slice: x: 4, y: 8, z: 8 (z_hi: 2, z_lo: 4; z = z_hi * 4 + z_lo), core: 2. Of those that a mesh axis runs over, the one named last changes fastest.
Arguments:
- psi: float32 [16, 2, 1024, 16, 512], P('al', None, 'row'), may hold values from -6 to 6
- angular: int32 [16, 16], replicated, may hold values from 0 to 15, each once within a row
- widths: int32 [32], P('row'), may hold values from 2 to 5
- field: float32 [1], replicated, may hold values from 0.2 to 0.6
- elem_matrix: bfloat16 [32, 32], replicated, may hold values from -1 to 1
- outer_matrix: bfloat16 [512, 512], replicated, may hold values from -1 to 1
Outputs:
- advanced: float32 [16, 2, 1024, 16, 512], P('al', None, 'row')
The draws below stay inside these ranges and needn't reach their ends.
Inputs may be any that keep to these rules, and one draw needn't show every extreme that they name: `angular`: each row holds every value 0 to 15 once.
All inputs are finite; a program needn't handle non-finite values.
Results may differ from the reference program's by a relative error of at most 0.0013.
Values sent between devices are 32-bit elements; how exact they have to be, the bound alone decides.
A program may use at most 128 MiB of HBM per device.

```python
import jax
import jax.numpy as jnp
from jax import lax

P_SIZE = 32
L2 = 16
R2 = 512
ORDER = 4
STEPS = 1
L1 = 16
ELEMS = 32
NR1 = 1024


def build_matrix(key, count):
    first_key, second_key = jax.random.split(jax.random.fold_in(key, 17), 2)
    diag = jax.random.uniform(first_key, (count,), jnp.float32, 0.6, 1.0)
    off = jax.random.uniform(second_key, (count, count), jnp.float32, -1.0, 1.0) * 0.6 / jnp.sqrt(count * 1.0)
    eye = jnp.eye(count, dtype=jnp.float32)
    return jnp.clip(off * (1.0 - eye) + diag[:, None] * eye, -1.0, 1.0)


def draw_elem_matrix(key, part):
    return build_matrix(jax.random.fold_in(key, 3), P_SIZE).astype(jnp.bfloat16)


def draw_outer_matrix(key, part):
    return build_matrix(jax.random.fold_in(key, 5), R2).astype(jnp.bfloat16)


def place_ends(values, stream_key, least, high):
    dims = values.shape
    spot = [jax.random.randint(jax.random.fold_in(stream_key, axis), (), 0, dims[axis]) for axis in range(len(dims))]
    values = values.at[tuple(spot)].set(least)
    longest = dims.index(max(dims))
    spot[longest] = (spot[longest] + 1) % dims[longest]
    return values.at[tuple(spot)].set(high)


def shard_levels(key, shape, cuts, low, top_value):
    def one(position, shards_of):
        draws = jax.random.uniform(jax.random.fold_in(jax.random.fold_in(key, 6), position), (shards_of,), jnp.float32, low / len(cuts), top_value / len(cuts))
        return jnp.repeat(jnp.exp(draws), shape[position] // shards_of).reshape((-1,) + (1,) * (len(shape) - position - 1))

    loudness = one(*cuts[0])
    for cut in cuts[1:]:
        loudness = loudness * one(*cut)
    return loudness


def gaussian(stream_key, shape, width, most, cuts=(), kind=jnp.bfloat16):
    entries = jax.random.normal(stream_key, shape, jnp.float32) * width
    if len(cuts) > 0:
        entries = shard_levels(stream_key, shape, cuts, -0.22, 0.18) * entries
    return jnp.clip(entries, min=-most, max=most).astype(kind)


def setup_inputs(seed: int = 0) -> dict:
    key_list = jax.random.split(jax.random.key(seed), 7)
    return {
        "psi": gaussian(key_list[0], (L1, 2, NR1, L2, R2), 1.0, 6.0, ((0, 16), (2, 32)), jnp.float32),
        "angular": jax.vmap(lambda own: jax.random.permutation(own, L2))(jax.random.split(key_list[1], L1)).reshape((L1, L2)).astype(jnp.int32),
        "widths": place_ends(jax.random.randint(key_list[2], (ELEMS,), 2, 6), jax.random.fold_in(key_list[2], 1), 2, 5).astype(jnp.int32),
        "field": jnp.clip(jax.random.uniform(key_list[3], (STEPS,), jnp.float32, 0.2, 0.6), 0.2, 0.6),
        "elem_matrix": draw_elem_matrix(jax.random.fold_in(key_list[6], 71), 0),
        "outer_matrix": draw_outer_matrix(jax.random.fold_in(key_list[6], 71), 0),
    }


dt_step = 0.35
radius_zero = 8.0
radial_step = 0.25
dipole_scale = 64.0

def coupling_weight(level):
    return (level + 1.0) / jnp.sqrt((2.0 * level + 1.0) * (2.0 * level + 3.0))

def reference(psi, angular, widths, field, elem_matrix, outer_matrix):
    edges = (jnp.cumsum(widths) - widths).astype(jnp.float32)
    nodes = jnp.arange(P_SIZE).astype(jnp.float32) / (P_SIZE - 1)
    wide = widths.astype(jnp.float32)
    radius_one = (radius_zero + edges[:, None] + wide[:, None] * nodes[None, :]).reshape(-1)
    scales = 4.0 / (wide * wide)
    radius_two = radius_zero + radial_step * jnp.arange(R2).astype(jnp.float32)
    first_matrix = elem_matrix.astype(jnp.float32)
    second_matrix = outer_matrix.astype(jnp.float32)
    repulsion = 1.0 / jnp.maximum(radius_one[:, None], radius_two[None, :])

    def potential(level, values):
        cent_one = level * (level + 1.0) / (2.0 * radius_one * radius_one) - 2.0 / radius_one
        cent_two = values[:, None] * (values[:, None] + 1.0) / (2.0 * radius_two[None, :] ** 2) - 2.0 / radius_two[None, :]
        return cent_one[:, None, None] + cent_two[None] + repulsion[:, None, :]

    def apply_ham(state, pot):
        rounded = state.astype(jnp.bfloat16)
        rounded = lax.optimization_barrier(rounded).astype(jnp.float32)
        inner = jnp.einsum('ik,cekm->ceim', first_matrix, rounded.reshape(2, ELEMS, P_SIZE, L2 * R2), precision=lax.Precision.HIGHEST) * scales[None, :, None, None]
        outer = jnp.einsum('cnk,kj->cnj', rounded.reshape(2, NR1 * L2, R2), second_matrix, precision=lax.Precision.HIGHEST)
        total = inner.reshape(state.shape) + outer.reshape(state.shape) + pot[None] * state
        blocks = total.reshape(2, ELEMS, P_SIZE, L2, R2)
        first = blocks[:, :, 0]
        last = blocks[:, :, P_SIZE - 1]
        joined = first[:, 1:] + last[:, :-1]
        zeros = jnp.zeros_like(first[:, :1])
        blocks = blocks.at[:, :, 0].set(jnp.concatenate([zeros, joined], 1))
        blocks = blocks.at[:, :, P_SIZE - 1].set(jnp.concatenate([joined, zeros], 1))
        return blocks.reshape(state.shape)
    for repeat in range(STEPS):
        strength = field[repeat]
        current = psi

        def advance(level_index):
            level = level_index.astype(jnp.float32)
            own = lax.dynamic_index_in_dim(current, level_index, 0, keepdims=False)
            own_perm = lax.dynamic_index_in_dim(angular, level_index, 0, keepdims=False)
            pot = potential(level, own_perm.astype(jnp.float32))
            term = own
            accum = own
            for power in range(1, ORDER + 1):
                image = apply_ham(term, pot)
                factor = dt_step / power
                term = jnp.stack([factor * image[1], -factor * image[0]])
                accum = accum + term
            below_index = jnp.maximum(level_index - 1, 0).astype(jnp.int32)
            above_index = jnp.minimum(level_index + 1, L1 - 1).astype(jnp.int32)
            below = lax.dynamic_index_in_dim(current, below_index, 0, keepdims=False)
            above = lax.dynamic_index_in_dim(current, above_index, 0, keepdims=False)
            perm_below = lax.dynamic_index_in_dim(angular, below_index, 0, keepdims=False)
            perm_above = lax.dynamic_index_in_dim(angular, above_index, 0, keepdims=False)
            match_below = (own_perm[:, None] == perm_below[None, :]).astype(jnp.float32)
            match_above = (own_perm[:, None] == perm_above[None, :]).astype(jnp.float32)
            has_below = (level_index > 0).astype(jnp.float32)
            has_above = (level_index < L1 - 1).astype(jnp.float32)
            mixed = coupling_weight(jnp.maximum(level - 1.0, 0.0)) * has_below * jnp.einsum('sq,cnqj->cnsj', match_below, below, precision=lax.Precision.HIGHEST)
            mixed = mixed + coupling_weight(level) * has_above * jnp.einsum('sq,cnqj->cnsj', match_above, above, precision=lax.Precision.HIGHEST)
            reach = (strength * radius_one / dipole_scale)[None, :, None, None]
            return jnp.stack([accum[0] + reach[0] * mixed[1], accum[1] - reach[0] * mixed[0]])
        psi = lax.map(advance, jnp.arange(L1, dtype=jnp.int32))
    return psi
```

```python
import functools

import jax
import jax.numpy as jnp
from jax import lax
from jax.experimental import pallas as pl
from jax.experimental.pallas import tpu as pltpu
from jax.sharding import PartitionSpec as P

MESH = pl.DeviceIdType.MESH
F32 = jnp.float32
BF16 = jnp.bfloat16

P_SIZE = 32
L2 = 16
R2 = 512
ORDER = 4
SUB = 8
GROUPS = L2 // SUB
ROWS = P_SIZE * SUB
QUAD = 4
CHUNKS = 4
CHUNK = P_SIZE // CHUNKS
MIXROWS = CHUNK * L2

dt_step = 0.35
radius_zero = 8.0
radial_step = 0.25
dipole_scale = 64.0


def iota(shape, dim):
    return lax.broadcasted_iota(jnp.int32, shape, dim)


def dot(a, b):
    return jnp.dot(a, b, preferred_element_type=F32)


def dot_lhs_t(a, b):
    return lax.dot_general(a, b, (((0,), (0,)), ((), ())), preferred_element_type=F32)


def ones_where(mask):
    return jnp.where(mask, 1.0, 0.0).astype(BF16)


def spread(size, inner, count):
    rows = iota((size, count), 0)
    rows = rows // inner if inner else rows % count
    return ones_where(rows == iota((size, count), 1))


def spread_t(size, inner, count):
    cols = iota((count, size), 1)
    cols = cols // inner if inner else cols % count
    return ones_where(cols == iota((count, size), 0))


def coupling_weight(level):
    return (level + 1.0) / jnp.sqrt((2.0 * level + 1.0) * (2.0 * level + 3.0))


def kernel(
    al_size, row_size,
    psi, ang, widths, field, elem, outer_hbm,
    out,
    xs, xbs, pot, below, above, outer_m, ke, kp, mix, cent2, potn, reach,
    psi_rim, rim_in, rim_out, op, partial, w_own, w_quad, w_total, w_ys,
    local_sem, bulk_send, bulk_recv, rim_send, rim_recv, psi_send, psi_recv, w_send, w_recv,
):
    a = lax.axis_index("al")
    r = lax.axis_index("row")
    quads = row_size // QUAD
    q = r % QUAD
    y = r // QUAD
    has_al = (a > 0, a < al_size - 1)
    has_row = (r > 0, r < row_size - 1)

    fetch_psi = pltpu.make_async_copy(psi, xs.at[0], local_sem.at[0])
    fetch_acc = pltpu.make_async_copy(psi, out, local_sem.at[1])
    fetch_outer = pltpu.make_async_copy(outer_hbm, outer_m, local_sem.at[2])
    fetch_psi.start()
    fetch_outer.start()
    fetch_acc.start()

    barrier = pltpu.get_barrier_semaphore()
    quad_peers = [y * QUAD + (q + j) % QUAD for j in range(1, QUAD)]
    y_peers = [((y + j) % quads) * QUAD + q for j in range(1, quads)]
    for peer in quad_peers + y_peers:
        pl.semaphore_signal(barrier, inc=1, device_id={"row": peer}, device_id_type=MESH)
    for side in range(2):
        step = 2 * side - 1

        @pl.when(has_al[side])
        def _():
            pl.semaphore_signal(barrier, inc=1, device_id={"al": a + step}, device_id_type=MESH)

        @pl.when(has_row[side])
        def _():
            pl.semaphore_signal(barrier, inc=1, device_id={"row": r + step}, device_id_type=MESH)

    w_own[...] = jnp.full((8, 128), widths[0], jnp.int32)
    wide = jnp.full((8, 128), widths[0], jnp.int32).astype(F32)
    scale = jnp.max(4.0 / (wide * wide))
    ef = elem[...].astype(F32)
    ri, ci = iota((P_SIZE, P_SIZE), 0), iota((P_SIZE, P_SIZE), 1)
    ends = (0, P_SIZE - 1)
    corner = [[jnp.sum(jnp.where((ri == i) & (ci == k), ef, 0.0)) * scale for k in ends] for i in ends]
    wide_rows = dot(spread(ROWS, SUB, P_SIZE), elem[...]).astype(BF16)
    kron = dot(wide_rows, spread_t(ROWS, SUB, P_SIZE))
    kr, kc = iota((ROWS, ROWS), 0), iota((ROWS, ROWS), 1)
    kron = jnp.where(kr % SUB == kc % SUB, kron, 0.0)
    ke[...] = kron.astype(BF16)
    inside = (kc >= SUB) & (kc < ROWS - SUB)
    kron = jnp.where(inside, kron, 0.0)
    kp[...] = jnp.concatenate([kron[0:SUB], kron[ROWS - SUB :]], 0).astype(BF16)

    angf = ang[...]
    slots = iota((L2, L2), 0)

    def one_hot(level):
        row = jnp.sum(jnp.where(slots == level, angf, 0), axis=0, keepdims=True)
        return ones_where(jnp.broadcast_to(row, (L2, L2)) == slots)

    own_hot = one_hot(a)
    mr, mc = iota((MIXROWS, MIXROWS), 0), iota((MIXROWS, MIXROWS), 1)
    for side in range(2):
        level = jnp.clip(a + 2 * side - 1, 0, al_size - 1)
        match = dot_lhs_t(own_hot, one_hot(level)).astype(BF16)
        tall = dot(spread(MIXROWS, 0, L2), match).astype(BF16)
        full = dot(tall, spread_t(MIXROWS, 0, L2))
        mix[side] = jnp.where(mr // L2 == mc // L2, full, 0.0).astype(BF16)
    momenta = iota((L2, R2), 0)
    square = dot_lhs_t(own_hot, (momenta * (momenta + 1)).astype(F32).astype(BF16))
    radius_two = radius_zero + radial_step * iota((L2, R2), 1).astype(F32)
    cent = square / (2.0 * radius_two * radius_two) - 2.0 / radius_two
    cent2[...] = cent.reshape(GROUPS, SUB, R2)

    level_one = jnp.full((8, 128), a, jnp.int32).astype(F32)
    weights = (
        jnp.max(coupling_weight(jnp.maximum(level_one - 1.0, 0.0))),
        jnp.max(coupling_weight(level_one)),
    )
    for side, buf in enumerate((below, above)):

        @pl.when(jnp.logical_not(has_al[side]))
        def _():
            def clear(n, _):
                for part in range(2):
                    buf[part, n] = jnp.zeros((GROUPS, SUB, R2), F32)
                return 0

            lax.fori_loop(0, P_SIZE, clear, 0)

    fetch_psi.wait()
    fetch_outer.wait()

    def partial_sums(slot, block):
        sums = dot(kp[...], xbs[slot, block]) * scale
        partial[0, block] = sums[0:SUB]
        partial[1, block] = sums[SUB:]

    def round_start(block, _):
        c, g = block // GROUPS, block % GROUPS
        xbs[0, block] = xs[0, c, :, g].reshape(ROWS, R2).astype(BF16)
        partial_sums(0, block)
        return 0

    lax.fori_loop(0, 2 * GROUPS, round_start, 0)

    def rim_rounded(slot, c, end):
        return xs[slot, c, ends[end]].astype(BF16).astype(F32)

    def rim_copy(k, side):
        return pltpu.make_async_remote_copy(
            src_ref=rim_out.at[k, side],
            dst_ref=rim_in.at[k, 1 - side],
            send_sem=rim_send.at[k, side],
            recv_sem=rim_recv.at[k, 1 - side],
            device_id={"row": r + 2 * side - 1},
            device_id_type=MESH,
        )

    def rim_arrival(k, side):
        return pltpu.make_async_remote_copy(
            src_ref=rim_out.at[k, 1 - side],
            dst_ref=rim_in.at[k, side],
            send_sem=rim_send.at[k, 1 - side],
            recv_sem=rim_recv.at[k, side],
            device_id={"row": r + 2 * side - 1},
            device_id_type=MESH,
        )

    def psi_copy(side):
        return pltpu.make_async_remote_copy(
            src_ref=psi.at[:, ends[side]],
            dst_ref=psi_rim.at[1 - side],
            send_sem=psi_send.at[side],
            recv_sem=psi_recv.at[1 - side],
            device_id={"row": r + 2 * side - 1},
            device_id_type=MESH,
        )

    def psi_arrival(side):
        return pltpu.make_async_remote_copy(
            src_ref=psi.at[:, ends[1 - side]],
            dst_ref=psi_rim.at[side],
            send_sem=psi_send.at[1 - side],
            recv_sem=psi_recv.at[side],
            device_id={"row": r + 2 * side - 1},
            device_id_type=MESH,
        )

    def rim_sums(k, slot):
        for c in range(2):
            low, high = rim_rounded(slot, c, 0), rim_rounded(slot, c, 1)
            for side in range(2):
                part = partial[side, c * GROUPS : (c + 1) * GROUPS]
                rim_out[k, side, c] = part + corner[side][0] * low + corner[side][1] * high

    def send_rims(k):
        for side in range(2):

            @pl.when(has_row[side])
            def _():
                rim_copy(k, side).start()

    bufs = (below, above)

    def bulk_copy(side, i):
        return pltpu.make_async_remote_copy(
            src_ref=psi.at[:, pl.ds(i * CHUNK, CHUNK)],
            dst_ref=bufs[1 - side].at[:, pl.ds(i * CHUNK, CHUNK)],
            send_sem=bulk_send.at[side, i],
            recv_sem=bulk_recv.at[1 - side, i],
            device_id={"al": a + 2 * side - 1},
            device_id_type=MESH,
        )

    def bulk_arrival(side, i):
        return pltpu.make_async_remote_copy(
            src_ref=psi.at[:, pl.ds(i * CHUNK, CHUNK)],
            dst_ref=bufs[side].at[:, pl.ds(i * CHUNK, CHUNK)],
            send_sem=bulk_send.at[1 - side, i],
            recv_sem=bulk_recv.at[side, i],
            device_id={"al": a + 2 * side - 1},
            device_id_type=MESH,
        )

    def width_copy(j, source, target, peer):
        return pltpu.make_async_remote_copy(
            src_ref=source,
            dst_ref=target,
            send_sem=w_send.at[j],
            recv_sem=w_recv.at[j],
            device_id={"row": peer},
            device_id_type=MESH,
        )

    quad_copies = [width_copy(j, w_own, w_quad.at[j], quad_peers[j]) for j in range(QUAD - 1)]
    y_copies = [
        width_copy(QUAD - 1 + j, w_total, w_ys.at[j], y_peers[j]) for j in range(quads - 1)
    ]

    rim_sums(0, 0)
    fetch_acc.wait()
    degree = QUAD - 1 + quads - 1
    for present in has_al + has_row:
        degree = degree + present.astype(jnp.int32)
    pl.semaphore_wait(barrier, degree)

    for copy in quad_copies:
        copy.start()
    for side in range(2):

        @pl.when(has_row[side])
        def _():
            psi_copy(side).start()

    send_rims(0)
    for i in range(CHUNKS):
        for side in range(2):

            @pl.when(has_al[side])
            def _():
                bulk_copy(side, i).start()

    total = w_own[...]
    lower = jnp.zeros((8, 128), jnp.int32)
    for j, copy in enumerate(quad_copies):
        copy.wait_recv()
        got = w_quad[j]
        total = total + got
        lower = lower + jnp.where((q + QUAD - 1 - j) % QUAD < q, got, 0)
    w_total[...] = total
    for copy in y_copies:
        copy.start()
    for j, copy in enumerate(y_copies):
        copy.wait_recv()
        lower = lower + jnp.where((y + quads - 1 - j) % quads < y, w_ys[j], 0)
    edge = lower.astype(F32)
    tile = (P_SIZE // 8, R2 // 128)
    nodes = iota((P_SIZE, R2), 0).astype(F32) / (P_SIZE - 1)
    radius_one = radius_zero + jnp.tile(edge, tile) + jnp.tile(wide, tile) * nodes
    radius_two = radius_zero + radial_step * iota((P_SIZE, R2), 1).astype(F32)
    level_rows = jnp.full((P_SIZE, R2), a, jnp.int32).astype(F32)
    cent_one = level_rows * (level_rows + 1.0) / (2.0 * radius_one * radius_one) - 2.0 / radius_one
    potn[...] = cent_one + 1.0 / jnp.maximum(radius_one, radius_two)
    reach[...] = field[0] * radius_one / dipole_scale

    def fill_pot(n, _):
        pot[n] = cent2[...] + potn[pl.ds(n, 1)][None]
        return 0

    lax.fori_loop(0, P_SIZE, fill_pot, 0)

    def blocks_of(k, old, new):
        factor = dt_step / k

        def one(block, _):
            c, g = block // GROUPS, block % GROUPS
            xb = xbs[old, block]
            inner = dot(ke[...], xb)
            outer = dot(xb, outer_m[...])
            rest = outer + pot[:, g].reshape(ROWS, R2) * xs[old, c, :, g].reshape(ROWS, R2)
            op[0, block] = rest[0:SUB]
            op[1, block] = rest[ROWS - SUB :]
            image = (inner * scale + rest) * jnp.where(c == 1, factor, -factor)
            d = 1 - c
            image3 = image.reshape(P_SIZE, SUB, R2)
            xs[new, d, :, g] = image3
            inner_planes = slice(1, P_SIZE - 1)
            out[d, inner_planes, g] = out[d, inner_planes, g] + image3[inner_planes]
            if k < ORDER:
                target = d * GROUPS + g
                xbs[new, target] = image.astype(BF16)
                partial_sums(new, target)
            return 0

        lax.fori_loop(0, 2 * GROUPS, one, 0)

    def mix_chunk(i):
        rows = pl.ds(i * CHUNK, CHUNK)

        def one(c, _):
            mixed = jnp.zeros((MIXROWS, R2), F32)
            for side in range(2):
                value = bufs[side][c, rows].reshape(MIXROWS, R2)
                high = value.astype(BF16)
                low = (value - high.astype(F32)).astype(BF16)
                mixed = mixed + weights[side] * (dot(mix[side], high) + dot(mix[side], low))
            sign = jnp.where(c == 1, 1.0, -1.0)
            mixed = mixed.reshape(CHUNK, GROUPS, SUB, R2)
            far = reach[rows][:, None, None, :] * sign
            out[1 - c, rows] = out[1 - c, rows] + far * mixed
            return 0

        lax.fori_loop(0, 2, one, 0)

    def receive_chunk(i):
        for side in range(2):

            @pl.when(has_al[side])
            def _():
                bulk_arrival(side, i).wait_recv()

        mix_chunk(i)

    def finish_rims(k, old, new):
        factor = dt_step / k
        for side in range(2):

            @pl.when(has_row[side])
            def _():
                rim_arrival(k - 1, side).wait_recv()

        for c in range(2):
            for side in range(2):
                mine = op[side, c * GROUPS : (c + 1) * GROUPS]
                if k == 1:
                    theirs = psi_op[side][c]
                else:
                    theirs = mine
                raw = (rim_out[k - 1, side, c] + rim_in[k - 1, side, c]) + (mine + theirs)
                raw = jnp.where(has_row[side], raw, 0.0)
                xs[new, 1 - c, ends[side]] = raw * (factor if c == 1 else -factor)
        if k < ORDER:
            rim_sums(k, new)
            send_rims(k)
        for c in range(2):
            for end in ends:
                out[c, end] = out[c, end] + xs[new, c, end]
            if k < ORDER:
                for g in range(GROUPS):
                    for first, place in ((0, 0), (P_SIZE - 2, ROWS - 2 * SUB)):
                        pair = xs[new, c, first : first + 2, g].reshape(2 * SUB, R2)
                        xbs[new, c * GROUPS + g, place : place + 2 * SUB] = pair.astype(BF16)

    blocks_of(1, 0, 1)
    psi_op = []
    for side in range(2):

        @pl.when(has_row[side])
        def _():
            psi_arrival(side).wait_recv()

        parts = []
        for c in range(2):
            other = psi_rim[side, c]
            there = dot(other.reshape(L2, R2).astype(BF16), outer_m[...])
            parts.append(there.reshape(GROUPS, SUB, R2) + pot[ends[side]] * other)
        psi_op.append(parts)
    finish_rims(1, 0, 1)
    for k in range(2, ORDER + 1):
        old, new = (k - 1) % 2, k % 2
        blocks_of(k, old, new)
        if k == 3:
            receive_chunk(0)
        if k == 4:
            receive_chunk(1)
        finish_rims(k, old, new)
    for i in range(2, CHUNKS):
        receive_chunk(i)

    for copy in quad_copies + y_copies:
        copy.wait_send()
    for side in range(2):

        @pl.when(has_row[side])
        def _():
            psi_copy(side).wait_send()
            for k in range(ORDER):
                rim_copy(k, side).wait_send()

        @pl.when(has_al[side])
        def _():
            for i in range(CHUNKS):
                bulk_copy(side, i).wait_send()


def local(al_size, row_size, psi, angular, widths, field, elem_matrix, outer_matrix):
    shape = (2, P_SIZE, GROUPS, SUB, R2)
    plane = (GROUPS, SUB, R2)
    quads = row_size // QUAD
    dma = pltpu.SemaphoreType.DMA
    vmem = pl.BlockSpec(memory_space=pltpu.VMEM)
    smem = pl.BlockSpec(memory_space=pltpu.SMEM)
    hbm = pl.BlockSpec(memory_space=pl.ANY)
    blocks = 2 * GROUPS
    advanced = pl.pallas_call(
        functools.partial(kernel, al_size, row_size),
        out_shape=jax.ShapeDtypeStruct(shape, F32),
        in_specs=[hbm, vmem, smem, smem, vmem, hbm],
        out_specs=vmem,
        scratch_shapes=[
            pltpu.VMEM((2,) + shape, F32),
            pltpu.VMEM((2, blocks, ROWS, R2), BF16),
            pltpu.VMEM((P_SIZE,) + plane, F32),
            pltpu.VMEM(shape, F32),
            pltpu.VMEM(shape, F32),
            pltpu.VMEM((R2, R2), BF16),
            pltpu.VMEM((ROWS, ROWS), BF16),
            pltpu.VMEM((2 * SUB, ROWS), BF16),
            pltpu.VMEM((2, MIXROWS, MIXROWS), BF16),
            pltpu.VMEM(plane, F32),
            pltpu.VMEM((P_SIZE, R2), F32),
            pltpu.VMEM((P_SIZE, R2), F32),
            pltpu.VMEM((2, 2) + plane, F32),
            pltpu.VMEM((ORDER, 2, 2) + plane, F32),
            pltpu.VMEM((ORDER, 2, 2) + plane, F32),
            pltpu.VMEM((2, blocks, SUB, R2), F32),
            pltpu.VMEM((2, blocks, SUB, R2), F32),
            pltpu.VMEM((8, 128), jnp.int32),
            pltpu.VMEM((QUAD - 1, 8, 128), jnp.int32),
            pltpu.VMEM((8, 128), jnp.int32),
            pltpu.VMEM((quads - 1, 8, 128), jnp.int32),
            dma((3,)),
            dma((2, CHUNKS)),
            dma((2, CHUNKS)),
            dma((ORDER, 2)),
            dma((ORDER, 2)),
            dma((2,)),
            dma((2,)),
            dma((QUAD + quads - 2,)),
            dma((QUAD + quads - 2,)),
        ],
        compiler_params=pltpu.CompilerParams(
            collective_id=0, has_side_effects=True, vmem_limit_bytes=48 * 1024 * 1024
        ),
    )(psi.reshape(shape), angular, widths, field, elem_matrix, outer_matrix)
    return advanced.reshape(psi.shape)


def solution(mesh):
    placed = (P("al", None, "row", None, None), P(), P("row"), P(), P(), P())
    return jax.shard_map(
        functools.partial(local, mesh.shape["al"], mesh.shape["row"]),
        mesh=mesh,
        in_specs=placed,
        out_specs=P("al", None, "row", None, None),
        check_vma=False,
    )
```

```python
import functools

import jax
import jax.numpy as jnp
from jax import lax
from jax.experimental import pallas as pl
from jax.experimental.pallas import tpu as pltpu
from jax.sharding import PartitionSpec as P

MESH = pl.DeviceIdType.MESH
F32 = jnp.float32
BF16 = jnp.bfloat16

P_SIZE = 32
L2 = 16
R2 = 512
ORDER = 4
SUB = 8
GROUPS = L2 // SUB
ROWS = P_SIZE * SUB
QUAD = 4
CHUNKS = 16
CHUNK = P_SIZE // CHUNKS
DIRECT = CHUNKS // 2
MIXPLANES = 8
MIXROWS = MIXPLANES * L2
X_SIZE = 4
PACE = 2

dt_step = 0.35
radius_zero = 8.0
radial_step = 0.25
dipole_scale = 64.0


def iota(shape, dim):
    return lax.broadcasted_iota(jnp.int32, shape, dim)


def dot(a, b):
    return jnp.dot(a, b, preferred_element_type=F32)


def dot_lhs_t(a, b):
    return lax.dot_general(a, b, (((0,), (0,)), ((), ())), preferred_element_type=F32)


def ones_where(mask):
    return jnp.where(mask, 1.0, 0.0).astype(BF16)


def spread(size, inner, count):
    rows = iota((size, count), 0)
    rows = rows // inner if inner else rows % count
    return ones_where(rows == iota((size, count), 1))


def spread_t(size, inner, count):
    cols = iota((count, size), 1)
    cols = cols // inner if inner else cols % count
    return ones_where(cols == iota((count, size), 0))


def coupling_weight(level):
    return (level + 1.0) / jnp.sqrt((2.0 * level + 1.0) * (2.0 * level + 3.0))


def kernel(
    al_size, row_size,
    psi, ang_hbm, widths, field, elem_hbm, outer_hbm,
    out,
    xs, xbs, pot, below, above, outer_m, ke, kp, mix, cent2, potn, reach,
    psi_rim, rim_in, rim_out, op, partial, w_own, w_quad, w_total, w_ys, ang, elem, held,
    local_sem, bulk_send, bulk_recv, rim_send, rim_recv, psi_send, psi_recv, w_send, w_recv,
    held_recv, pass_send,
):
    a = lax.axis_index("al")
    r = lax.axis_index("row")
    quads = row_size // QUAD
    q = r % QUAD
    y = r // QUAD
    x = a % X_SIZE
    has_al = (a > 0, a < al_size - 1)
    wraps = (has_al[0] & (x == 0), has_al[1] & (x == X_SIZE - 1))
    at_end = (x == 0) | (x == X_SIZE - 1)
    inward = jnp.where(x == 0, 1, -1)
    passes = at_end & (a + inward * X_SIZE >= 0) & (a + inward * X_SIZE < al_size)
    pass_from = a + inward * (X_SIZE - 1)
    pass_to = a + inward * X_SIZE
    pass_side = (passes & (x == X_SIZE - 1), passes & (x == 0))
    al_peers = [
        (has_al[0], a - 1),
        (has_al[1], a + 1),
        (at_end & (a >= X_SIZE), a - X_SIZE),
        (at_end & (a < al_size - X_SIZE), a + X_SIZE),
        (at_end, a + inward * (X_SIZE - 1)),
    ]
    has_row = (r > 0, r < row_size - 1)

    fetch_psi = pltpu.make_async_copy(psi, xs.at[0], local_sem.at[0])
    fetch_acc = pltpu.make_async_copy(psi, out, local_sem.at[1])
    fetch_outer = pltpu.make_async_copy(outer_hbm, outer_m, local_sem.at[2])
    fetch_small = [
        pltpu.make_async_copy(elem_hbm, elem, local_sem.at[3]),
        pltpu.make_async_copy(ang_hbm, ang, local_sem.at[4]),
    ]
    for fetch in fetch_small:
        fetch.start()
    fetch_psi.start()
    fetch_outer.start()
    fetch_acc.start()

    barrier = pltpu.get_barrier_semaphore()
    quad_peers = [y * QUAD + (q + j) % QUAD for j in range(1, QUAD)]
    y_peers = [((y + j) % quads) * QUAD + q for j in range(1, quads)]
    for peer in quad_peers + y_peers:
        pl.semaphore_signal(barrier, inc=1, device_id={"row": peer}, device_id_type=MESH)
    for side in range(2):
        step = 2 * side - 1

        @pl.when(has_row[side])
        def _():
            pl.semaphore_signal(barrier, inc=1, device_id={"row": r + step}, device_id_type=MESH)

    for present, peer in al_peers:

        @pl.when(present)
        def _():
            pl.semaphore_signal(barrier, inc=1, device_id={"al": peer}, device_id_type=MESH)

    w_own[...] = jnp.full((8, 128), widths[0], jnp.int32)
    wide = jnp.full((8, 128), widths[0], jnp.int32).astype(F32)
    scale = jnp.max(4.0 / (wide * wide))
    for fetch in fetch_small:
        fetch.wait()
    ef = elem[...].astype(F32)
    ri, ci = iota((P_SIZE, P_SIZE), 0), iota((P_SIZE, P_SIZE), 1)
    ends = (0, P_SIZE - 1)
    corner = [[jnp.sum(jnp.where((ri == i) & (ci == k), ef, 0.0)) * scale for k in ends] for i in ends]
    wide_rows = dot(spread(ROWS, SUB, P_SIZE), elem[...]).astype(BF16)
    kron = dot(wide_rows, spread_t(ROWS, SUB, P_SIZE))
    kr, kc = iota((ROWS, ROWS), 0), iota((ROWS, ROWS), 1)
    kron = jnp.where(kr % SUB == kc % SUB, kron, 0.0)
    ke[...] = kron.astype(BF16)
    inside = (kc >= SUB) & (kc < ROWS - SUB)
    kron = jnp.where(inside, kron, 0.0)
    kp[...] = jnp.concatenate([kron[0:SUB], kron[ROWS - SUB :]], 0).astype(BF16)

    angf = ang[...]
    slots = iota((L2, L2), 0)

    def one_hot(level):
        row = jnp.sum(jnp.where(slots == level, angf, 0), axis=0, keepdims=True)
        return ones_where(jnp.broadcast_to(row, (L2, L2)) == slots)

    own_hot = one_hot(a)
    mr, mc = iota((MIXROWS, MIXROWS), 0), iota((MIXROWS, MIXROWS), 1)
    for side in range(2):
        level = jnp.clip(a + 2 * side - 1, 0, al_size - 1)
        match = dot_lhs_t(own_hot, one_hot(level)).astype(BF16)
        tall = dot(spread(MIXROWS, 0, L2), match).astype(BF16)
        full = dot(tall, spread_t(MIXROWS, 0, L2))
        mix[side] = jnp.where(mr // L2 == mc // L2, full, 0.0).astype(BF16)
    momenta = iota((L2, R2), 0)
    square = dot_lhs_t(own_hot, (momenta * (momenta + 1)).astype(F32).astype(BF16))
    radius_two = radius_zero + radial_step * iota((L2, R2), 1).astype(F32)
    cent = square / (2.0 * radius_two * radius_two) - 2.0 / radius_two
    cent2[...] = cent.reshape(GROUPS, SUB, R2)

    level_one = jnp.full((8, 128), a, jnp.int32).astype(F32)
    weights = (
        jnp.max(coupling_weight(jnp.maximum(level_one - 1.0, 0.0))),
        jnp.max(coupling_weight(level_one)),
    )
    for side, buf in enumerate((below, above)):

        @pl.when(jnp.logical_not(has_al[side]))
        def _():
            def clear(n, _):
                for part in range(2):
                    buf[part, n] = jnp.zeros((GROUPS, SUB, R2), F32)
                return 0

            lax.fori_loop(0, P_SIZE, clear, 0)

    fetch_psi.wait()
    fetch_outer.wait()

    def partial_sums(slot, block):
        sums = dot(kp[...], xbs[slot, block]) * scale
        partial[0, block] = sums[0:SUB]
        partial[1, block] = sums[SUB:]

    def round_start(block, _):
        c, g = block // GROUPS, block % GROUPS
        xbs[0, block] = xs[0, c, :, g].reshape(ROWS, R2).astype(BF16)
        partial_sums(0, block)
        return 0

    lax.fori_loop(0, 2 * GROUPS, round_start, 0)

    def rim_rounded(slot, c, end):
        return xs[slot, c, ends[end]].astype(BF16).astype(F32)

    def rim_copy(k, side):
        return pltpu.make_async_remote_copy(
            src_ref=rim_out.at[k, side],
            dst_ref=rim_in.at[k, 1 - side],
            send_sem=rim_send.at[k, side],
            recv_sem=rim_recv.at[k, 1 - side],
            device_id={"row": r + 2 * side - 1},
            device_id_type=MESH,
        )

    def rim_arrival(k, side):
        return pltpu.make_async_remote_copy(
            src_ref=rim_out.at[k, 1 - side],
            dst_ref=rim_in.at[k, side],
            send_sem=rim_send.at[k, 1 - side],
            recv_sem=rim_recv.at[k, side],
            device_id={"row": r + 2 * side - 1},
            device_id_type=MESH,
        )

    def psi_copy(side):
        return pltpu.make_async_remote_copy(
            src_ref=psi.at[:, ends[side]],
            dst_ref=psi_rim.at[1 - side],
            send_sem=psi_send.at[side],
            recv_sem=psi_recv.at[1 - side],
            device_id={"row": r + 2 * side - 1},
            device_id_type=MESH,
        )

    def psi_arrival(side):
        return pltpu.make_async_remote_copy(
            src_ref=psi.at[:, ends[1 - side]],
            dst_ref=psi_rim.at[side],
            send_sem=psi_send.at[1 - side],
            recv_sem=psi_recv.at[side],
            device_id={"row": r + 2 * side - 1},
            device_id_type=MESH,
        )

    def rim_sums(k, slot):
        for c in range(2):
            low, high = rim_rounded(slot, c, 0), rim_rounded(slot, c, 1)
            for side in range(2):
                part = partial[side, c * GROUPS : (c + 1) * GROUPS]
                rim_out[k, side, c] = part + corner[side][0] * low + corner[side][1] * high

    def send_rims(k):
        for side in range(2):

            @pl.when(has_row[side])
            def _():
                rim_copy(k, side).start()

    bufs = (below, above)

    def bulk_copy(side, i):
        return pltpu.make_async_remote_copy(
            src_ref=psi.at[:, pl.ds(i * CHUNK, CHUNK)],
            dst_ref=bufs[1 - side].at[:, pl.ds(i * CHUNK, CHUNK)],
            send_sem=bulk_send.at[side, i],
            recv_sem=bulk_recv.at[1 - side, i],
            device_id={"al": a + 2 * side - 1},
            device_id_type=MESH,
        )

    def relay_copy(side, i):
        ahead = (2 * side - 1) * (1 - X_SIZE)
        return pltpu.make_async_remote_copy(
            src_ref=psi.at[:, pl.ds(i * CHUNK, CHUNK)],
            dst_ref=held.at[i - DIRECT],
            send_sem=bulk_send.at[side, i],
            recv_sem=held_recv.at[i - DIRECT],
            device_id={"al": a + ahead},
            device_id_type=MESH,
        )

    def pass_copy(side, i):
        return pltpu.make_async_remote_copy(
            src_ref=held.at[i - DIRECT],
            dst_ref=bufs[1 - side].at[:, pl.ds(i * CHUNK, CHUNK)],
            send_sem=pass_send.at[i - DIRECT],
            recv_sem=bulk_recv.at[1 - side, i],
            device_id={"al": pass_to},
            device_id_type=MESH,
        )

    def pass_on(turn):
        for i in range(DIRECT + PACE * turn, DIRECT + PACE * (turn + 1)):

            @pl.when(passes)
            def _():
                pltpu.make_async_remote_copy(
                    src_ref=psi.at[:, pl.ds(i * CHUNK, CHUNK)],
                    dst_ref=held.at[i - DIRECT],
                    send_sem=bulk_send.at[0, i],
                    recv_sem=held_recv.at[i - DIRECT],
                    device_id={"al": pass_from},
                    device_id_type=MESH,
                ).wait_recv()

            for side in range(2):

                @pl.when(pass_side[side])
                def _():
                    pass_copy(side, i).start()

    def start_bulk():
        for side in range(2):

            @pl.when(has_al[side] & jnp.logical_not(wraps[side]))
            def _():
                for i in range(CHUNKS):
                    bulk_copy(side, i).start()

            @pl.when(wraps[side])
            def _():
                for i in range(DIRECT, CHUNKS):
                    relay_copy(side, i).start()

    def start_direct(turn):
        for side in range(2):

            @pl.when(wraps[side])
            def _():
                for i in range(PACE * turn, PACE * (turn + 1)):
                    bulk_copy(side, i).start()

    def bulk_arrival(side, i):
        return pltpu.make_async_remote_copy(
            src_ref=psi.at[:, pl.ds(i * CHUNK, CHUNK)],
            dst_ref=bufs[side].at[:, pl.ds(i * CHUNK, CHUNK)],
            send_sem=bulk_send.at[1 - side, i],
            recv_sem=bulk_recv.at[side, i],
            device_id={"al": a + 2 * side - 1},
            device_id_type=MESH,
        )

    def width_copy(j, source, target, peer):
        return pltpu.make_async_remote_copy(
            src_ref=source,
            dst_ref=target,
            send_sem=w_send.at[j],
            recv_sem=w_recv.at[j],
            device_id={"row": peer},
            device_id_type=MESH,
        )

    quad_copies = [width_copy(j, w_own, w_quad.at[j], quad_peers[j]) for j in range(QUAD - 1)]
    y_copies = [
        width_copy(QUAD - 1 + j, w_total, w_ys.at[j], y_peers[j]) for j in range(quads - 1)
    ]

    rim_sums(0, 0)
    fetch_acc.wait()
    degree = QUAD - 1 + quads - 1
    for present in [present for present, _ in al_peers] + list(has_row):
        degree = degree + present.astype(jnp.int32)
    pl.semaphore_wait(barrier, degree)

    for copy in quad_copies:
        copy.start()
    for side in range(2):

        @pl.when(has_row[side])
        def _():
            psi_copy(side).start()

    send_rims(0)
    start_bulk()
    start_direct(0)

    total = w_own[...]
    lower = jnp.zeros((8, 128), jnp.int32)
    for j, copy in enumerate(quad_copies):
        copy.wait_recv()
        got = w_quad[j]
        total = total + got
        lower = lower + jnp.where((q + QUAD - 1 - j) % QUAD < q, got, 0)
    w_total[...] = total
    for copy in y_copies:
        copy.start()
    for j, copy in enumerate(y_copies):
        copy.wait_recv()
        lower = lower + jnp.where((y + quads - 1 - j) % quads < y, w_ys[j], 0)
    edge = lower.astype(F32)
    tile = (P_SIZE // 8, R2 // 128)
    nodes = iota((P_SIZE, R2), 0).astype(F32) / (P_SIZE - 1)
    radius_one = radius_zero + jnp.tile(edge, tile) + jnp.tile(wide, tile) * nodes
    radius_two = radius_zero + radial_step * iota((P_SIZE, R2), 1).astype(F32)
    level_rows = jnp.full((P_SIZE, R2), a, jnp.int32).astype(F32)
    cent_one = level_rows * (level_rows + 1.0) / (2.0 * radius_one * radius_one) - 2.0 / radius_one
    potn[...] = cent_one + 1.0 / jnp.maximum(radius_one, radius_two)
    reach[...] = field[0] * radius_one / dipole_scale

    def fill_pot(n, _):
        pot[n] = cent2[...] + potn[pl.ds(n, 1)][None]
        return 0

    lax.fori_loop(0, P_SIZE, fill_pot, 0)

    def blocks_of(k, old, new):
        factor = dt_step / k

        def one(block, _):
            c, g = block // GROUPS, block % GROUPS
            xb = xbs[old, block]
            inner = dot(ke[...], xb)
            outer = dot(xb, outer_m[...])
            rest = outer + pot[:, g].reshape(ROWS, R2) * xs[old, c, :, g].reshape(ROWS, R2)
            op[0, block] = rest[0:SUB]
            op[1, block] = rest[ROWS - SUB :]
            image = (inner * scale + rest) * jnp.where(c == 1, factor, -factor)
            d = 1 - c
            image3 = image.reshape(P_SIZE, SUB, R2)
            xs[new, d, :, g] = image3
            inner_planes = slice(1, P_SIZE - 1)
            out[d, inner_planes, g] = out[d, inner_planes, g] + image3[inner_planes]
            if k < ORDER:
                target = d * GROUPS + g
                xbs[new, target] = image.astype(BF16)
                partial_sums(new, target)
            return 0

        lax.fori_loop(0, 2 * GROUPS, one, 0)

    def mix_planes(first, count):
        rows = pl.ds(first, count)
        size = count * L2

        def one(c, _):
            mixed = jnp.zeros((size, R2), F32)
            for side in range(2):
                value = bufs[side][c, rows].reshape(size, R2)
                high = value.astype(BF16)
                low = (value - high.astype(F32)).astype(BF16)
                match = mix[side, 0:size, 0:size]
                mixed = mixed + weights[side] * (dot(match, high) + dot(match, low))
            sign = jnp.where(c == 1, 1.0, -1.0)
            mixed = mixed.reshape(count, GROUPS, SUB, R2)
            far = reach[rows][:, None, None, :] * sign
            out[1 - c, rows] = out[1 - c, rows] + far * mixed
            return 0

        lax.fori_loop(0, 2, one, 0)

    def receive_planes(first, count):
        for i in range(first // CHUNK, (first + count) // CHUNK):
            for side in range(2):

                @pl.when(has_al[side])
                def _():
                    bulk_arrival(side, i).wait_recv()

        mix_planes(first, count)

    def finish_rims(k, old, new):
        factor = dt_step / k
        for side in range(2):

            @pl.when(has_row[side])
            def _():
                rim_arrival(k - 1, side).wait_recv()

        for c in range(2):
            for side in range(2):
                mine = op[side, c * GROUPS : (c + 1) * GROUPS]
                if k == 1:
                    theirs = psi_op[side][c]
                else:
                    theirs = mine
                raw = (rim_out[k - 1, side, c] + rim_in[k - 1, side, c]) + (mine + theirs)
                raw = jnp.where(has_row[side], raw, 0.0)
                xs[new, 1 - c, ends[side]] = raw * (factor if c == 1 else -factor)
        if k < ORDER:
            rim_sums(k, new)
            send_rims(k)
        for c in range(2):
            for end in ends:
                out[c, end] = out[c, end] + xs[new, c, end]
            if k < ORDER:
                for g in range(GROUPS):
                    for first, place in ((0, 0), (P_SIZE - 2, ROWS - 2 * SUB)):
                        pair = xs[new, c, first : first + 2, g].reshape(2 * SUB, R2)
                        xbs[new, c * GROUPS + g, place : place + 2 * SUB] = pair.astype(BF16)

    blocks_of(1, 0, 1)
    psi_op = []
    for side in range(2):

        @pl.when(has_row[side])
        def _():
            psi_arrival(side).wait_recv()

        parts = []
        for c in range(2):
            other = psi_rim[side, c]
            there = dot(other.reshape(L2, R2).astype(BF16), outer_m[...])
            parts.append(there.reshape(GROUPS, SUB, R2) + pot[ends[side]] * other)
        psi_op.append(parts)
    finish_rims(1, 0, 1)
    for k in range(2, ORDER + 1):
        start_direct(k - 1)
        pass_on(k - 2)
        old, new = (k - 1) % 2, k % 2
        blocks_of(k, old, new)
        if k == 4:
            receive_planes(0, 8)
        finish_rims(k, old, new)
    pass_on(ORDER - 1)
    receive_planes(8, 8)
    receive_planes(16, 8)
    receive_planes(24, 4)
    receive_planes(28, 4)

    for copy in quad_copies + y_copies:
        copy.wait_send()
    for side in range(2):

        @pl.when(has_row[side])
        def _():
            psi_copy(side).wait_send()
            for k in range(ORDER):
                rim_copy(k, side).wait_send()

        @pl.when(has_al[side])
        def _():
            for i in range(CHUNKS):
                bulk_copy(side, i).wait_send()

        @pl.when(pass_side[side])
        def _():
            for i in range(DIRECT, CHUNKS):
                pass_copy(side, i).wait_send()


def local(al_size, row_size, psi, angular, widths, field, elem_matrix, outer_matrix):
    shape = (2, P_SIZE, GROUPS, SUB, R2)
    plane = (GROUPS, SUB, R2)
    quads = row_size // QUAD
    dma = pltpu.SemaphoreType.DMA
    vmem = pl.BlockSpec(memory_space=pltpu.VMEM)
    smem = pl.BlockSpec(memory_space=pltpu.SMEM)
    hbm = pl.BlockSpec(memory_space=pltpu.HBM)
    blocks = 2 * GROUPS
    advanced = pl.pallas_call(
        functools.partial(kernel, al_size, row_size),
        out_shape=jax.ShapeDtypeStruct(shape, F32),
        in_specs=[hbm, hbm, smem, smem, hbm, hbm],
        out_specs=vmem,
        scratch_shapes=[
            pltpu.VMEM((2,) + shape, F32),
            pltpu.VMEM((2, blocks, ROWS, R2), BF16),
            pltpu.VMEM((P_SIZE,) + plane, F32),
            pltpu.VMEM(shape, F32),
            pltpu.VMEM(shape, F32),
            pltpu.VMEM((R2, R2), BF16),
            pltpu.VMEM((ROWS, ROWS), BF16),
            pltpu.VMEM((2 * SUB, ROWS), BF16),
            pltpu.VMEM((2, MIXROWS, MIXROWS), BF16),
            pltpu.VMEM(plane, F32),
            pltpu.VMEM((P_SIZE, R2), F32),
            pltpu.VMEM((P_SIZE, R2), F32),
            pltpu.VMEM((2, 2) + plane, F32),
            pltpu.VMEM((ORDER, 2, 2) + plane, F32),
            pltpu.VMEM((ORDER, 2, 2) + plane, F32),
            pltpu.VMEM((2, blocks, SUB, R2), F32),
            pltpu.VMEM((2, blocks, SUB, R2), F32),
            pltpu.VMEM((8, 128), jnp.int32),
            pltpu.VMEM((QUAD - 1, 8, 128), jnp.int32),
            pltpu.VMEM((8, 128), jnp.int32),
            pltpu.VMEM((quads - 1, 8, 128), jnp.int32),
            pltpu.VMEM((L2, L2), jnp.int32),
            pltpu.VMEM((P_SIZE, P_SIZE), BF16),
            pltpu.VMEM((CHUNKS - DIRECT, 2, CHUNK) + plane, F32),
            dma((5,)),
            dma((2, CHUNKS)),
            dma((2, CHUNKS)),
            dma((ORDER, 2)),
            dma((ORDER, 2)),
            dma((2,)),
            dma((2,)),
            dma((QUAD + quads - 2,)),
            dma((QUAD + quads - 2,)),
            dma((CHUNKS - DIRECT,)),
            dma((CHUNKS - DIRECT,)),
        ],
        compiler_params=pltpu.CompilerParams(
            collective_id=0, has_side_effects=True, vmem_limit_bytes=48 * 1024 * 1024
        ),
    )(*[pltpu.with_memory_space_constraint(v, pltpu.HBM) if i in (0,1,4,5) else v for i,v in enumerate((psi.reshape(shape), angular, widths, field, elem_matrix, outer_matrix))])
    return advanced.reshape(psi.shape)


def solution(mesh):
    placed = (P("al", None, "row", None, None), P(), P("row"), P(), P(), P())
    return jax.shard_map(
        functools.partial(local, mesh.shape["al"], mesh.shape["row"]),
        mesh=mesh,
        in_specs=placed,
        out_specs=P("al", None, "row", None, None),
        check_vma=False,
    )
```

```python
import functools

import jax
import jax.numpy as jnp
from jax import lax
from jax.experimental import pallas as pl
from jax.experimental.pallas import tpu as pltpu
from jax.sharding import PartitionSpec as P

MESH = pl.DeviceIdType.MESH
F32 = jnp.float32
BF16 = jnp.bfloat16

P_SIZE = 32
L2 = 16
R2 = 512
ORDER = 4
SUB = 8
GROUPS = L2 // SUB
ROWS = P_SIZE * SUB
QUAD = 4
CHUNKS = P_SIZE
CHUNK = P_SIZE // CHUNKS
DIRECT = CHUNKS // 2
MIXPLANES = 8
MIXROWS = MIXPLANES * L2
X_SIZE = 4
CHAINS = 2 * GROUPS
BIG = 4

dt_step = 0.35
radius_zero = 8.0
radial_step = 0.25
dipole_scale = 64.0


def iota(shape, dim):
    return lax.broadcasted_iota(jnp.int32, shape, dim)


def dot(a, b):
    return jnp.dot(a, b, preferred_element_type=F32)


def dot_lhs_t(a, b):
    return lax.dot_general(a, b, (((0,), (0,)), ((), ())), preferred_element_type=F32)


def ones_where(mask):
    return jnp.where(mask, 1.0, 0.0).astype(BF16)


def spread(size, inner, count):
    rows = iota((size, count), 0)
    rows = rows // inner if inner else rows % count
    return ones_where(rows == iota((size, count), 1))


def spread_t(size, inner, count):
    cols = iota((count, size), 1)
    cols = cols // inner if inner else cols % count
    return ones_where(cols == iota((count, size), 0))


def coupling_weight(level):
    return (level + 1.0) / jnp.sqrt((2.0 * level + 1.0) * (2.0 * level + 3.0))


def kernel(
    al_size, row_size,
    psi, ang_hbm, widths, field, elem_hbm, outer_hbm,
    out,
    xs, xbs, pot, below, above, outer_m, ke, kp, mix, cent2, potn, reach,
    psi_rim, rim_in, rim_out, op, op_there, partial, w_own, w_quad, w_total, w_ys, ang, elem, held, held_z,
    local_sem, bulk_send, bulk_recv, rim_send, rim_recv, psi_send, psi_recv, w_send, w_recv,
    held_recv, pass_send, held_z_recv, pass_z_send,
    near_sem, twice_sem, row_sem,
):
    a = lax.axis_index("al")
    r = lax.axis_index("row")
    quads = row_size // QUAD
    q = r % QUAD
    y = r // QUAD
    x = a % X_SIZE
    has_al = (a > 0, a < al_size - 1)
    wraps = (has_al[0] & (x == 0), has_al[1] & (x == X_SIZE - 1))
    at_end = (x == 0) | (x == X_SIZE - 1)
    inward = jnp.where(x == 0, 1, -1)
    passes = at_end & (a + inward * X_SIZE >= 0) & (a + inward * X_SIZE < al_size)
    pass_from = a + inward * (X_SIZE - 1)
    pass_to = a + inward * X_SIZE
    pass_side = (passes & (x == X_SIZE - 1), passes & (x == 0))
    pass_z_side = (pass_side[1], pass_side[0])
    has_row = (r > 0, r < row_size - 1)
    odd = x % 2 == 1
    even = jnp.logical_not(odd)
    al_peers = [(has_al[0], a - 1), (has_al[1], a + 1), (at_end, a + inward * (X_SIZE - 1))]

    fetch_psi = pltpu.make_async_copy(psi, xs.at[0], local_sem.at[0])
    fetch_acc = pltpu.make_async_copy(psi, out, local_sem.at[1])
    fetch_outer = pltpu.make_async_copy(outer_hbm, outer_m, local_sem.at[2])
    fetch_small = [
        pltpu.make_async_copy(elem_hbm, elem, local_sem.at[3]),
        pltpu.make_async_copy(ang_hbm, ang, local_sem.at[4]),
    ]
    for fetch in fetch_small:
        fetch.start()
    fetch_psi.start()
    fetch_outer.start()
    fetch_acc.start()

    barrier = pltpu.get_barrier_semaphore()
    quad_peers = [y * QUAD + (q + j) % QUAD for j in range(1, QUAD)]
    y_peers = [((y + j) % quads) * QUAD + q for j in range(1, quads)]

    def signal_al(sem):
        for present, peer in al_peers:

            @pl.when(present)
            def _():
                pl.semaphore_signal(sem, inc=1, device_id={"al": peer}, device_id_type=MESH)

    al_count = 0
    for present, _ in al_peers:
        al_count = al_count + present.astype(jnp.int32)
    row_count = QUAD - 1 + quads - 1
    for present in has_row:
        row_count = row_count + present.astype(jnp.int32)

    @pl.when(odd)
    def _():
        signal_al(barrier)

    w_own[...] = jnp.full((8, 128), widths[0], jnp.int32)
    ends = (0, P_SIZE - 1)

    def partial_sums(xb, chain):
        sums = dot(kp[...], xb) * scale
        partial[0, chain] = sums[0:SUB]
        partial[1, chain] = sums[SUB:]

    def round_start(chain, _):
        c, g = chain // GROUPS, chain % GROUPS
        xb = xs[0, c, :, g].reshape(ROWS, R2).astype(BF16)
        xbs[0, chain] = xb
        partial_sums(xb, chain)
        rim_sums(0, chain, [xs[0, c, end, g] for end in ends])
        return 0

    def rim_copy(k, side, chain):
        return pltpu.make_async_remote_copy(
            src_ref=rim_out.at[k, side, chain],
            dst_ref=rim_in.at[k, 1 - side, chain],
            send_sem=rim_send.at[k, side, chain],
            recv_sem=rim_recv.at[k, 1 - side, chain],
            device_id={"row": r + 2 * side - 1},
            device_id_type=MESH,
        )

    def rim_arrival(k, side, chain):
        return pltpu.make_async_remote_copy(
            src_ref=rim_out.at[k, 1 - side, chain],
            dst_ref=rim_in.at[k, side, chain],
            send_sem=rim_send.at[k, 1 - side, chain],
            recv_sem=rim_recv.at[k, side, chain],
            device_id={"row": r + 2 * side - 1},
            device_id_type=MESH,
        )

    def psi_copy(side):
        return pltpu.make_async_remote_copy(
            src_ref=psi.at[:, ends[side]],
            dst_ref=psi_rim.at[1 - side],
            send_sem=psi_send.at[side],
            recv_sem=psi_recv.at[1 - side],
            device_id={"row": r + 2 * side - 1},
            device_id_type=MESH,
        )

    def psi_arrival(side):
        return pltpu.make_async_remote_copy(
            src_ref=psi.at[:, ends[1 - side]],
            dst_ref=psi_rim.at[side],
            send_sem=psi_send.at[1 - side],
            recv_sem=psi_recv.at[side],
            device_id={"row": r + 2 * side - 1},
            device_id_type=MESH,
        )

    def rim_sums(k, chain, rims):
        rounded = [rim.astype(BF16).astype(F32) for rim in rims]
        for side in range(2):
            lows, highs = [corner[side][end] * rounded[end] for end in range(2)]
            rim_out[k, side, chain] = partial[side, chain] + lows + highs

    def send_rims(k, chain):
        for side in range(2):

            @pl.when(has_row[side])
            def _():
                rim_copy(k, side, chain).start()

    bufs = (below, above)

    def bulk_copy(side, j):
        return pltpu.make_async_remote_copy(
            src_ref=psi.at[:, pl.ds(j * BIG, BIG)],
            dst_ref=bufs[1 - side].at[:, pl.ds(j * BIG, BIG)],
            send_sem=bulk_send.at[side, j],
            recv_sem=bulk_recv.at[1 - side, j],
            device_id={"al": a + 2 * side - 1},
            device_id_type=MESH,
        )

    def relay_copy(side, i):
        ahead = (2 * side - 1) * (1 - X_SIZE)
        return pltpu.make_async_remote_copy(
            src_ref=psi.at[:, pl.ds(i * CHUNK, CHUNK)],
            dst_ref=held.at[i - DIRECT],
            send_sem=bulk_send.at[side, i],
            recv_sem=held_recv.at[i - DIRECT],
            device_id={"al": a + ahead},
            device_id_type=MESH,
        )

    def pass_copy(side, i):
        return pltpu.make_async_remote_copy(
            src_ref=held.at[i - DIRECT],
            dst_ref=bufs[1 - side].at[:, pl.ds(i * CHUNK, CHUNK)],
            send_sem=pass_send.at[i - DIRECT],
            recv_sem=bulk_recv.at[1 - side, i],
            device_id={"al": pass_to},
            device_id_type=MESH,
        )

    def pass_on(i):
        @pl.when(passes)
        def _():
            pltpu.make_async_remote_copy(
                src_ref=psi.at[:, pl.ds(i * CHUNK, CHUNK)],
                dst_ref=held.at[i - DIRECT],
                send_sem=bulk_send.at[0, i],
                recv_sem=held_recv.at[i - DIRECT],
                device_id={"al": pass_from},
                device_id_type=MESH,
            ).wait_recv()

        for side in range(2):

            @pl.when(pass_side[side])
            def _():
                pass_copy(side, i).start()

    def ahead_copy(side, i):
        return pltpu.make_async_remote_copy(
            src_ref=psi.at[:, pl.ds(i * CHUNK, CHUNK)],
            dst_ref=held_z.at[i],
            send_sem=bulk_send.at[side, i],
            recv_sem=held_z_recv.at[i],
            device_id={"al": a + (2 * side - 1) * X_SIZE},
            device_id_type=MESH,
        )

    def pass_z_copy(side, i):
        return pltpu.make_async_remote_copy(
            src_ref=held_z.at[i],
            dst_ref=bufs[1 - side].at[:, pl.ds(i * CHUNK, CHUNK)],
            send_sem=pass_z_send.at[i],
            recv_sem=bulk_recv.at[1 - side, i],
            device_id={"al": pass_from},
            device_id_type=MESH,
        )

    def pass_z_on(i):
        @pl.when(passes)
        def _():
            pltpu.make_async_remote_copy(
                src_ref=psi.at[:, pl.ds(i * CHUNK, CHUNK)],
                dst_ref=held_z.at[i],
                send_sem=bulk_send.at[0, i],
                recv_sem=held_z_recv.at[i],
                device_id={"al": pass_to},
                device_id_type=MESH,
            ).wait_recv()

        for side in range(2):

            @pl.when(pass_z_side[side])
            def _():
                pass_z_copy(side, i).start()

    def over(first, last, act):
        def one(i, _):
            act(i)
            return 0

        lax.fori_loop(first, last, one, 0)

    def relay_part(side):
        def act(i):
            @pl.when(i >= DIRECT)
            def _():
                relay_copy(side, i).start()

        return act

    def start_pieces(j):
        for side in range(2):

            @pl.when(has_al[side] & jnp.logical_not(wraps[side]))
            def _():
                bulk_copy(side, j).start()

            @pl.when(wraps[side])
            def _():
                over(j * BIG, (j + 1) * BIG, relay_part(side))

    def start_ahead(i):
        for side in range(2):

            @pl.when(wraps[side])
            def _():
                ahead_copy(side, i).start()

    def arrival(side, first, count, sem):
        return pltpu.make_async_remote_copy(
            src_ref=psi.at[:, pl.ds(first, count)],
            dst_ref=bufs[side].at[:, pl.ds(first, count)],
            send_sem=bulk_send.at[1 - side, sem],
            recv_sem=bulk_recv.at[side, sem],
            device_id={"al": a + 2 * side - 1},
            device_id_type=MESH,
        )

    def width_copy(j, source, target, peer):
        return pltpu.make_async_remote_copy(
            src_ref=source,
            dst_ref=target,
            send_sem=w_send.at[j],
            recv_sem=w_recv.at[j],
            device_id={"row": peer},
            device_id_type=MESH,
        )

    quad_copies = [width_copy(j, w_own, w_quad.at[j], quad_peers[j]) for j in range(QUAD - 1)]
    y_copies = [
        width_copy(QUAD - 1 + j, w_total, w_ys.at[j], y_peers[j]) for j in range(quads - 1)
    ]

    @pl.when(even)
    def _():
        pl.semaphore_wait(barrier, al_count)
        signal_al(near_sem)

    @pl.when(odd)
    def _():
        pl.semaphore_wait(near_sem, al_count)
        signal_al(twice_sem)
        for peer in quad_peers + y_peers:
            pl.semaphore_signal(barrier, inc=1, device_id={"row": peer}, device_id_type=MESH)
        for side in range(2):

            @pl.when(has_row[side])
            def _():
                pl.semaphore_signal(
                    barrier, inc=1, device_id={"row": r + 2 * side - 1}, device_id_type=MESH
                )

    over(DIRECT // BIG, CHUNKS // BIG, start_pieces)
    over(0, DIRECT // BIG, start_pieces)

    @pl.when(even)
    def _():
        pl.semaphore_wait(twice_sem, al_count)

    over(0, 4, start_ahead)

    wide = jnp.full((8, 128), widths[0], jnp.int32).astype(F32)
    scale = jnp.max(4.0 / (wide * wide))
    for fetch in fetch_small:
        fetch.wait()
    ef = elem[...].astype(F32)
    ri, ci = iota((P_SIZE, P_SIZE), 0), iota((P_SIZE, P_SIZE), 1)
    corner = [[jnp.sum(jnp.where((ri == i) & (ci == k), ef, 0.0)) * scale for k in ends] for i in ends]
    wide_rows = dot(spread(ROWS, SUB, P_SIZE), elem[...]).astype(BF16)
    kron = dot(wide_rows, spread_t(ROWS, SUB, P_SIZE))
    kr, kc = iota((ROWS, ROWS), 0), iota((ROWS, ROWS), 1)
    kron = jnp.where(kr % SUB == kc % SUB, kron, 0.0)
    ke[...] = kron.astype(BF16)
    inside = (kc >= SUB) & (kc < ROWS - SUB)
    kron = jnp.where(inside, kron, 0.0)
    kp[...] = jnp.concatenate([kron[0:SUB], kron[ROWS - SUB :]], 0).astype(BF16)

    fetch_psi.wait()
    fetch_outer.wait()

    over(0, CHAINS, lambda chain: round_start(chain, 0))

    @pl.when(odd)
    def _():
        pl.semaphore_wait(barrier, row_count)
        pl.semaphore_signal(row_sem, inc=1, device_id={"al": a - 1}, device_id_type=MESH)

    @pl.when(even)
    def _():
        pl.semaphore_wait(row_sem, 1)

    for copy in quad_copies:
        copy.start()
    for side in range(2):

        @pl.when(has_row[side])
        def _():
            psi_copy(side).start()

    over(0, CHAINS, lambda chain: send_rims(0, chain))
    over(4, 7, start_ahead)
    over(DIRECT, DIRECT + 3, pass_on)

    angf = ang[...]
    slots = iota((L2, L2), 0)

    def one_hot(level):
        row = jnp.sum(jnp.where(slots == level, angf, 0), axis=0, keepdims=True)
        return ones_where(jnp.broadcast_to(row, (L2, L2)) == slots)

    own_hot = one_hot(a)
    mr, mc = iota((MIXROWS, MIXROWS), 0), iota((MIXROWS, MIXROWS), 1)
    for side in range(2):
        level = jnp.clip(a + 2 * side - 1, 0, al_size - 1)
        match = dot_lhs_t(own_hot, one_hot(level)).astype(BF16)
        tall = dot(spread(MIXROWS, 0, L2), match).astype(BF16)
        full = dot(tall, spread_t(MIXROWS, 0, L2))
        mix[side] = jnp.where(mr // L2 == mc // L2, full, 0.0).astype(BF16)
    momenta = iota((L2, R2), 0)
    square = dot_lhs_t(own_hot, (momenta * (momenta + 1)).astype(F32).astype(BF16))
    radius_two = radius_zero + radial_step * iota((L2, R2), 1).astype(F32)
    cent = square / (2.0 * radius_two * radius_two) - 2.0 / radius_two
    cent2[...] = cent.reshape(GROUPS, SUB, R2)

    level_one = jnp.full((8, 128), a, jnp.int32).astype(F32)
    weights = (
        jnp.max(coupling_weight(jnp.maximum(level_one - 1.0, 0.0))),
        jnp.max(coupling_weight(level_one)),
    )
    for side, buf in enumerate((below, above)):

        @pl.when(jnp.logical_not(has_al[side]))
        def _():
            def clear(n, _):
                for part in range(2):
                    buf[part, n] = jnp.zeros((GROUPS, SUB, R2), F32)
                return 0

            lax.fori_loop(0, P_SIZE, clear, 0)

    fetch_acc.wait()

    total = w_own[...]
    lower = jnp.zeros((8, 128), jnp.int32)
    for j, copy in enumerate(quad_copies):
        copy.wait_recv()
        got = w_quad[j]
        total = total + got
        lower = lower + jnp.where((q + QUAD - 1 - j) % QUAD < q, got, 0)
    w_total[...] = total
    for copy in y_copies:
        copy.start()
    for j, copy in enumerate(y_copies):
        copy.wait_recv()
        lower = lower + jnp.where((y + quads - 1 - j) % quads < y, w_ys[j], 0)
    over(0, 4, pass_z_on)
    edge = lower.astype(F32)
    tile = (P_SIZE // 8, R2 // 128)
    nodes = iota((P_SIZE, R2), 0).astype(F32) / (P_SIZE - 1)
    radius_one = radius_zero + jnp.tile(edge, tile) + jnp.tile(wide, tile) * nodes
    radius_two = radius_zero + radial_step * iota((P_SIZE, R2), 1).astype(F32)
    level_rows = jnp.full((P_SIZE, R2), a, jnp.int32).astype(F32)
    cent_one = level_rows * (level_rows + 1.0) / (2.0 * radius_one * radius_one) - 2.0 / radius_one
    potn[...] = cent_one + 1.0 / jnp.maximum(radius_one, radius_two)
    reach[...] = field[0] * radius_one / dipole_scale

    def fill_pot(n, _):
        pot[n] = cent2[...] + potn[pl.ds(n, 1)][None]
        return 0

    lax.fori_loop(0, P_SIZE, fill_pot, 0)

    def place(k, chain):
        return (chain // GROUPS + k) % 2, chain % GROUPS

    def inside_of(k, chain):
        old, new = (k - 1) % 2, k % 2
        factor = dt_step / k
        c, g = place(k - 1, chain)
        d = 1 - c
        xb = xbs[old, c * GROUPS + g]
        inner = dot(ke[...], xb)
        outer = dot(xb, outer_m[...])
        rest = outer + pot[:, g].reshape(ROWS, R2) * xs[old, c, :, g].reshape(ROWS, R2)
        op[0, chain] = rest[0:SUB]
        op[1, chain] = rest[ROWS - SUB :]
        image = (inner * scale + rest) * jnp.where(c == 1, factor, -factor)
        image3 = image.reshape(P_SIZE, SUB, R2)
        xs[new, d, :, g] = image3
        inner_planes = slice(1, P_SIZE - 1)
        out[d, inner_planes, g] = out[d, inner_planes, g] + image3[inner_planes]
        if k < ORDER:
            xb = image.astype(BF16)
            xbs[new, d * GROUPS + g] = xb
            partial_sums(xb, chain)

    def rims_of(k, chain):
        new = k % 2
        factor = dt_step / k
        c, g = place(k - 1, chain)
        d = 1 - c
        for side in range(2):

            @pl.when(has_row[side])
            def _():
                rim_arrival(k - 1, side, chain).wait_recv()

        rims = []
        for side in range(2):
            mine = op[side, chain]
            theirs = op_there[side, chain] if k == 1 else mine
            raw = (rim_out[k - 1, side, chain] + rim_in[k - 1, side, chain]) + (mine + theirs)
            raw = jnp.where(has_row[side], raw, 0.0)
            rims.append(raw * jnp.where(c == 1, factor, -factor))
        if k < ORDER:
            rim_sums(k, chain, rims)
            send_rims(k, chain)
        for rim, end in zip(rims, ends):
            xs[new, d, end, g] = rim
            out[d, end, g] = out[d, end, g] + rim
        if k < ORDER:
            for first, row in ((0, 0), (P_SIZE - 2, ROWS - 2 * SUB)):
                pair = xs[new, d, first : first + 2, g].reshape(2 * SUB, R2)
                xbs[new, d * GROUPS + g, row : row + 2 * SUB] = pair.astype(BF16)

    def mix_planes(first, count):
        rows = pl.ds(first, count)
        size = count * L2

        def one(c, _):
            mixed = jnp.zeros((size, R2), F32)
            for side in range(2):
                value = bufs[side][c, rows].reshape(size, R2)
                high = value.astype(BF16)
                low = (value - high.astype(F32)).astype(BF16)
                match = mix[side, 0:size, 0:size]
                mixed = mixed + weights[side] * (dot(match, high) + dot(match, low))
            sign = jnp.where(c == 1, 1.0, -1.0)
            mixed = mixed.reshape(count, GROUPS, SUB, R2)
            far = reach[rows][:, None, None, :] * sign
            out[1 - c, rows] = out[1 - c, rows] + far * mixed
            return 0

        lax.fori_loop(0, 2, one, 0)

    def receive_planes(first, count):
        for side in range(2):

            @pl.when(has_al[side] & jnp.logical_not(wraps[side]))
            def _():
                for j in range(first // BIG, (first + count) // BIG):
                    arrival(side, j * BIG, BIG, j).wait_recv()

            @pl.when(wraps[side])
            def _():
                over(first, first + count, lambda i: arrival(side, i, 1, i).wait_recv())

        mix_planes(first, count)

    for side in range(2):

        @pl.when(has_row[side])
        def _():
            psi_arrival(side).wait_recv()

    beyond = psi_rim[...]
    there = dot(beyond.reshape(2 * 2 * L2, R2).astype(BF16), outer_m[...])
    there = there.reshape(2, 2, GROUPS, SUB, R2)
    for side in range(2):
        added = there[side] + pot[ends[side]][None] * beyond[side]
        op_there[side] = added.reshape(CHAINS, SUB, R2)

    over(0, CHAINS, lambda chain: inside_of(1, chain))
    plan = (
        (start_ahead, (7, 9, 10, DIRECT)),
        (pass_on, (DIRECT + 3, DIRECT + 5, DIRECT + 7, CHUNKS)),
        (pass_z_on, (4, 6, 8, 10)),
    )
    for k in range(1, ORDER + 1):

        def step(chain):
            turn = CHAINS * (k - 1) + chain
            rims_of(k, chain)

            if k < ORDER:

                @pl.when(chain == CHAINS - 1)
                def _():
                    for act, bounds in plan:
                        over(bounds[k - 1], bounds[k], act)

            if k < ORDER:
                inside_of(k + 1, chain)

        over(0, CHAINS, step)
    over(10, 14, pass_z_on)
    receive_planes(16, 8)
    over(14, DIRECT, pass_z_on)
    for first, count in ((24, 8), (0, 8), (8, 4), (12, 4)):
        receive_planes(first, count)

    for copy in quad_copies + y_copies:
        copy.wait_send()
    for side in range(2):

        @pl.when(has_row[side])
        def _():
            psi_copy(side).wait_send()
            for k in range(ORDER):
                over(0, CHAINS, lambda chain: rim_copy(k, side, chain).wait_send())

        @pl.when(has_al[side] & jnp.logical_not(wraps[side]))
        def _():
            over(0, CHUNKS // BIG, lambda j: bulk_copy(side, j).wait_send())

        @pl.when(wraps[side])
        def _():
            over(DIRECT, CHUNKS, lambda i: relay_copy(side, i).wait_send())
            over(0, DIRECT, lambda i: ahead_copy(side, i).wait_send())

        @pl.when(pass_side[side])
        def _():
            over(DIRECT, CHUNKS, lambda i: pass_copy(side, i).wait_send())

        @pl.when(pass_z_side[side])
        def _():
            over(0, DIRECT, lambda i: pass_z_copy(side, i).wait_send())


def local(al_size, row_size, psi, angular, widths, field, elem_matrix, outer_matrix):
    shape = (2, P_SIZE, GROUPS, SUB, R2)
    plane = (GROUPS, SUB, R2)
    in_hbm = functools.partial(pltpu.with_memory_space_constraint, memory_space=pltpu.HBM)
    quads = row_size // QUAD
    dma = pltpu.SemaphoreType.DMA
    vmem = pl.BlockSpec(memory_space=pltpu.VMEM)
    smem = pl.BlockSpec(memory_space=pltpu.SMEM)
    hbm = pl.BlockSpec(memory_space=pltpu.HBM)
    advanced = pl.pallas_call(
        functools.partial(kernel, al_size, row_size),
        out_shape=jax.ShapeDtypeStruct(shape, F32),
        in_specs=[hbm, hbm, smem, smem, hbm, hbm],
        out_specs=vmem,
        scratch_shapes=[
            pltpu.VMEM((2,) + shape, F32),
            pltpu.VMEM((2, CHAINS, ROWS, R2), BF16),
            pltpu.VMEM((P_SIZE,) + plane, F32),
            pltpu.VMEM(shape, F32),
            pltpu.VMEM(shape, F32),
            pltpu.VMEM((R2, R2), BF16),
            pltpu.VMEM((ROWS, ROWS), BF16),
            pltpu.VMEM((2 * SUB, ROWS), BF16),
            pltpu.VMEM((2, MIXROWS, MIXROWS), BF16),
            pltpu.VMEM(plane, F32),
            pltpu.VMEM((P_SIZE, R2), F32),
            pltpu.VMEM((P_SIZE, R2), F32),
            pltpu.VMEM((2, 2) + plane, F32),
            pltpu.VMEM((ORDER, 2, CHAINS, SUB, R2), F32),
            pltpu.VMEM((ORDER, 2, CHAINS, SUB, R2), F32),
            pltpu.VMEM((2, CHAINS, SUB, R2), F32),
            pltpu.VMEM((2, CHAINS, SUB, R2), F32),
            pltpu.VMEM((2, CHAINS, SUB, R2), F32),
            pltpu.VMEM((8, 128), jnp.int32),
            pltpu.VMEM((QUAD - 1, 8, 128), jnp.int32),
            pltpu.VMEM((8, 128), jnp.int32),
            pltpu.VMEM((quads - 1, 8, 128), jnp.int32),
            pltpu.VMEM((L2, L2), jnp.int32),
            pltpu.VMEM((P_SIZE, P_SIZE), BF16),
            pltpu.VMEM((CHUNKS - DIRECT, 2, CHUNK) + plane, F32),
            pltpu.VMEM((DIRECT, 2, CHUNK) + plane, F32),
            dma((5,)),
            dma((2, CHUNKS)),
            dma((2, CHUNKS)),
            dma((ORDER, 2, CHAINS)),
            dma((ORDER, 2, CHAINS)),
            dma((2,)),
            dma((2,)),
            dma((QUAD + quads - 2,)),
            dma((QUAD + quads - 2,)),
            dma((CHUNKS - DIRECT,)),
            dma((CHUNKS - DIRECT,)),
            dma((DIRECT,)),
            dma((DIRECT,)),
            pltpu.SemaphoreType.REGULAR,
            pltpu.SemaphoreType.REGULAR,
            pltpu.SemaphoreType.REGULAR,
        ],
        compiler_params=pltpu.CompilerParams(
            collective_id=0, has_side_effects=True, vmem_limit_bytes=48 * 1024 * 1024
        ),
    )(
        in_hbm(psi.reshape(shape)),
        in_hbm(angular),
        widths,
        field,
        in_hbm(elem_matrix),
        in_hbm(outer_matrix),
    )
    return advanced.reshape(psi.shape)


def solution(mesh):
    placed = (P("al", None, "row", None, None), P(), P("row"), P(), P(), P())
    return jax.shard_map(
        functools.partial(local, mesh.shape["al"], mesh.shape["row"]),
        mesh=mesh,
        in_specs=placed,
        out_specs=P("al", None, "row", None, None),
        check_vma=False,
    )
```

```python
import functools

import jax
import jax.numpy as jnp
from jax import lax
from jax.experimental import pallas as pl
from jax.experimental.pallas import tpu as pltpu
from jax.sharding import PartitionSpec as P

MESH = pl.DeviceIdType.MESH
F32 = jnp.float32
BF16 = jnp.bfloat16

P_SIZE = 32
L2 = 16
R2 = 512
ORDER = 4
SUB = 8
GROUPS = L2 // SUB
ROWS = P_SIZE * SUB
QUAD = 4
CHUNKS = 16
CHUNK = P_SIZE // CHUNKS
DIRECT = 8
AHEAD = (0, 2, 3, 5, 8)
PASSED = (8, 9, 11, 13, 16)
MIXPLANES = 8
MIXROWS = MIXPLANES * L2
X_SIZE = 4

dt_step = 0.35
radius_zero = 8.0
radial_step = 0.25
dipole_scale = 64.0


def iota(shape, dim):
    return lax.broadcasted_iota(jnp.int32, shape, dim)


def dot(a, b):
    return jnp.dot(a, b, preferred_element_type=F32)


def dot_lhs_t(a, b):
    return lax.dot_general(a, b, (((0,), (0,)), ((), ())), preferred_element_type=F32)


def ones_where(mask):
    return jnp.where(mask, 1.0, 0.0).astype(BF16)


def spread(size, inner, count):
    rows = iota((size, count), 0)
    rows = rows // inner if inner else rows % count
    return ones_where(rows == iota((size, count), 1))


def spread_t(size, inner, count):
    cols = iota((count, size), 1)
    cols = cols // inner if inner else cols % count
    return ones_where(cols == iota((count, size), 0))


def coupling_weight(level):
    return (level + 1.0) / jnp.sqrt((2.0 * level + 1.0) * (2.0 * level + 3.0))


def kernel(
    al_size, row_size,
    psi, ang_hbm, widths, field, elem_hbm, outer_hbm,
    out,
    xs, xbs, pot, below, above, outer_m, ke, kp, mix, cent2, potn, reach,
    psi_rim, rim_in, rim_out, op, partial, w_own, w_quad, w_total, w_ys, ang, elem, held,
    local_sem, bulk_send, bulk_recv, rim_send, rim_recv, psi_send, psi_recv, w_send, w_recv,
    held_recv, pass_send, near_sem, twice_sem, row_sem,
):
    a = lax.axis_index("al")
    r = lax.axis_index("row")
    quads = row_size // QUAD
    q = r % QUAD
    y = r // QUAD
    x = a % X_SIZE
    has_al = (a > 0, a < al_size - 1)
    wraps = (has_al[0] & (x == 0), has_al[1] & (x == X_SIZE - 1))
    at_end = (x == 0) | (x == X_SIZE - 1)
    inward = jnp.where(x == 0, 1, -1)
    passes = at_end & (a + inward * X_SIZE >= 0) & (a + inward * X_SIZE < al_size)
    pass_from = a + inward * (X_SIZE - 1)
    pass_to = a + inward * X_SIZE
    pass_side = (passes & (x == X_SIZE - 1), passes & (x == 0))
    has_row = (r > 0, r < row_size - 1)
    odd = x % 2 == 1
    even = jnp.logical_not(odd)
    al_peers = [(has_al[0], a - 1), (has_al[1], a + 1), (at_end, a + inward * (X_SIZE - 1))]

    fetch_psi = pltpu.make_async_copy(psi, xs.at[0], local_sem.at[0])
    fetch_acc = pltpu.make_async_copy(psi, out, local_sem.at[1])
    fetch_outer = pltpu.make_async_copy(outer_hbm, outer_m, local_sem.at[2])
    fetch_small = [
        pltpu.make_async_copy(elem_hbm, elem, local_sem.at[3]),
        pltpu.make_async_copy(ang_hbm, ang, local_sem.at[4]),
    ]
    for fetch in fetch_small:
        fetch.start()
    fetch_psi.start()
    fetch_outer.start()
    fetch_acc.start()

    barrier = pltpu.get_barrier_semaphore()
    quad_peers = [y * QUAD + (q + j) % QUAD for j in range(1, QUAD)]
    y_peers = [((y + j) % quads) * QUAD + q for j in range(1, quads)]

    def signal_al(sem):
        for present, peer in al_peers:

            @pl.when(present)
            def _():
                pl.semaphore_signal(sem, inc=1, device_id={"al": peer}, device_id_type=MESH)

    al_count = 0
    for present, _ in al_peers:
        al_count = al_count + present.astype(jnp.int32)
    row_count = QUAD - 1 + quads - 1
    for present in has_row:
        row_count = row_count + present.astype(jnp.int32)

    @pl.when(odd)
    def _():
        signal_al(barrier)

    w_own[...] = jnp.full((8, 128), widths[0], jnp.int32)
    ends = (0, P_SIZE - 1)

    def rim_rounded(slot, c, end):
        return xs[slot, c, ends[end]].astype(BF16).astype(F32)

    def rim_copy(k, side):
        return pltpu.make_async_remote_copy(
            src_ref=rim_out.at[k, side],
            dst_ref=rim_in.at[k, 1 - side],
            send_sem=rim_send.at[k, side],
            recv_sem=rim_recv.at[k, 1 - side],
            device_id={"row": r + 2 * side - 1},
            device_id_type=MESH,
        )

    def rim_arrival(k, side):
        return pltpu.make_async_remote_copy(
            src_ref=rim_out.at[k, 1 - side],
            dst_ref=rim_in.at[k, side],
            send_sem=rim_send.at[k, 1 - side],
            recv_sem=rim_recv.at[k, side],
            device_id={"row": r + 2 * side - 1},
            device_id_type=MESH,
        )

    def psi_copy(side):
        return pltpu.make_async_remote_copy(
            src_ref=psi.at[:, ends[side]],
            dst_ref=psi_rim.at[1 - side],
            send_sem=psi_send.at[side],
            recv_sem=psi_recv.at[1 - side],
            device_id={"row": r + 2 * side - 1},
            device_id_type=MESH,
        )

    def psi_arrival(side):
        return pltpu.make_async_remote_copy(
            src_ref=psi.at[:, ends[1 - side]],
            dst_ref=psi_rim.at[side],
            send_sem=psi_send.at[1 - side],
            recv_sem=psi_recv.at[side],
            device_id={"row": r + 2 * side - 1},
            device_id_type=MESH,
        )

    def rim_sums(k, slot):
        for c in range(2):
            low, high = rim_rounded(slot, c, 0), rim_rounded(slot, c, 1)
            for side in range(2):
                part = partial[side, c * GROUPS : (c + 1) * GROUPS]
                rim_out[k, side, c] = part + corner[side][0] * low + corner[side][1] * high

    def send_rims(k):
        for side in range(2):

            @pl.when(has_row[side])
            def _():
                rim_copy(k, side).start()

    bufs = (below, above)

    def bulk_copy(side, i):
        return pltpu.make_async_remote_copy(
            src_ref=psi.at[:, pl.ds(i * CHUNK, CHUNK)],
            dst_ref=bufs[1 - side].at[:, pl.ds(i * CHUNK, CHUNK)],
            send_sem=bulk_send.at[side, i],
            recv_sem=bulk_recv.at[1 - side, i],
            device_id={"al": a + 2 * side - 1},
            device_id_type=MESH,
        )

    def relay_copy(side, i):
        ahead = (2 * side - 1) * (1 - X_SIZE)
        return pltpu.make_async_remote_copy(
            src_ref=psi.at[:, pl.ds(i * CHUNK, CHUNK)],
            dst_ref=held.at[i - DIRECT],
            send_sem=bulk_send.at[side, i],
            recv_sem=held_recv.at[i - DIRECT],
            device_id={"al": a + ahead},
            device_id_type=MESH,
        )

    def pass_copy(side, i):
        return pltpu.make_async_remote_copy(
            src_ref=held.at[i - DIRECT],
            dst_ref=bufs[1 - side].at[:, pl.ds(i * CHUNK, CHUNK)],
            send_sem=pass_send.at[i - DIRECT],
            recv_sem=bulk_recv.at[1 - side, i],
            device_id={"al": pass_to},
            device_id_type=MESH,
        )

    def pass_on(turn):
        for i in range(PASSED[turn], PASSED[turn + 1]):

            @pl.when(passes)
            def _():
                pltpu.make_async_remote_copy(
                    src_ref=psi.at[:, pl.ds(i * CHUNK, CHUNK)],
                    dst_ref=held.at[i - DIRECT],
                    send_sem=bulk_send.at[0, i],
                    recv_sem=held_recv.at[i - DIRECT],
                    device_id={"al": pass_from},
                    device_id_type=MESH,
                ).wait_recv()

            for side in range(2):

                @pl.when(pass_side[side])
                def _():
                    pass_copy(side, i).start()

    def start_bulk():
        for i in range(CHUNKS):
            for side in range(2):

                @pl.when(has_al[side] & jnp.logical_not(wraps[side]))
                def _():
                    bulk_copy(side, i).start()

                if i >= DIRECT:

                    @pl.when(wraps[side])
                    def _():
                        relay_copy(side, i).start()

    def start_direct(turn):
        for side in range(2):

            @pl.when(wraps[side])
            def _():
                for i in range(AHEAD[turn], AHEAD[turn + 1]):
                    bulk_copy(side, i).start()

    def bulk_arrival(side, i):
        return pltpu.make_async_remote_copy(
            src_ref=psi.at[:, pl.ds(i * CHUNK, CHUNK)],
            dst_ref=bufs[side].at[:, pl.ds(i * CHUNK, CHUNK)],
            send_sem=bulk_send.at[1 - side, i],
            recv_sem=bulk_recv.at[side, i],
            device_id={"al": a + 2 * side - 1},
            device_id_type=MESH,
        )

    def width_copy(j, source, target, peer):
        return pltpu.make_async_remote_copy(
            src_ref=source,
            dst_ref=target,
            send_sem=w_send.at[j],
            recv_sem=w_recv.at[j],
            device_id={"row": peer},
            device_id_type=MESH,
        )

    quad_copies = [width_copy(j, w_own, w_quad.at[j], quad_peers[j]) for j in range(QUAD - 1)]
    y_copies = [
        width_copy(QUAD - 1 + j, w_total, w_ys.at[j], y_peers[j]) for j in range(quads - 1)
    ]

    @pl.when(even)
    def _():
        pl.semaphore_wait(barrier, al_count)
        signal_al(near_sem)

    @pl.when(odd)
    def _():
        pl.semaphore_wait(near_sem, al_count)
        signal_al(twice_sem)
        for peer in quad_peers + y_peers:
            pl.semaphore_signal(barrier, inc=1, device_id={"row": peer}, device_id_type=MESH)
        for side in range(2):

            @pl.when(has_row[side])
            def _():
                pl.semaphore_signal(
                    barrier, inc=1, device_id={"row": r + 2 * side - 1}, device_id_type=MESH
                )

    start_bulk()

    start_direct(0)

    wide = jnp.full((8, 128), widths[0], jnp.int32).astype(F32)
    scale = jnp.max(4.0 / (wide * wide))
    for fetch in fetch_small:
        fetch.wait()
    ef = elem[...].astype(F32)
    ri, ci = iota((P_SIZE, P_SIZE), 0), iota((P_SIZE, P_SIZE), 1)
    corner = [[jnp.sum(jnp.where((ri == i) & (ci == k), ef, 0.0)) * scale for k in ends] for i in ends]
    wide_rows = dot(spread(ROWS, SUB, P_SIZE), elem[...]).astype(BF16)
    kron = dot(wide_rows, spread_t(ROWS, SUB, P_SIZE))
    kr, kc = iota((ROWS, ROWS), 0), iota((ROWS, ROWS), 1)
    kron = jnp.where(kr % SUB == kc % SUB, kron, 0.0)
    ke[...] = kron.astype(BF16)
    inside = (kc >= SUB) & (kc < ROWS - SUB)
    kron = jnp.where(inside, kron, 0.0)
    kp[...] = jnp.concatenate([kron[0:SUB], kron[ROWS - SUB :]], 0).astype(BF16)

    fetch_psi.wait()
    fetch_outer.wait()

    def partial_sums(slot, block):
        sums = dot(kp[...], xbs[slot, block]) * scale
        partial[0, block] = sums[0:SUB]
        partial[1, block] = sums[SUB:]

    def round_start(block, _):
        c, g = block // GROUPS, block % GROUPS
        xbs[0, block] = xs[0, c, :, g].reshape(ROWS, R2).astype(BF16)
        partial_sums(0, block)
        return 0

    lax.fori_loop(0, 2 * GROUPS, round_start, 0)

    rim_sums(0, 0)

    @pl.when(odd)
    def _():
        pl.semaphore_wait(barrier, row_count)
        pl.semaphore_signal(row_sem, inc=1, device_id={"al": a - 1}, device_id_type=MESH)

    @pl.when(even)
    def _():
        pl.semaphore_wait(row_sem, 1)

    for copy in quad_copies:
        copy.start()
    for side in range(2):

        @pl.when(has_row[side])
        def _():
            psi_copy(side).start()

    send_rims(0)
    start_direct(1)

    @pl.when(even)
    def _():
        pl.semaphore_wait(twice_sem, al_count)

    pass_on(0)
    angf = ang[...]
    slots = iota((L2, L2), 0)

    def one_hot(level):
        row = jnp.sum(jnp.where(slots == level, angf, 0), axis=0, keepdims=True)
        return ones_where(jnp.broadcast_to(row, (L2, L2)) == slots)

    own_hot = one_hot(a)
    mr, mc = iota((MIXROWS, MIXROWS), 0), iota((MIXROWS, MIXROWS), 1)
    for side in range(2):
        level = jnp.clip(a + 2 * side - 1, 0, al_size - 1)
        match = dot_lhs_t(own_hot, one_hot(level)).astype(BF16)
        tall = dot(spread(MIXROWS, 0, L2), match).astype(BF16)
        full = dot(tall, spread_t(MIXROWS, 0, L2))
        mix[side] = jnp.where(mr // L2 == mc // L2, full, 0.0).astype(BF16)
    momenta = iota((L2, R2), 0)
    square = dot_lhs_t(own_hot, (momenta * (momenta + 1)).astype(F32).astype(BF16))
    radius_two = radius_zero + radial_step * iota((L2, R2), 1).astype(F32)
    cent = square / (2.0 * radius_two * radius_two) - 2.0 / radius_two
    cent2[...] = cent.reshape(GROUPS, SUB, R2)

    level_one = jnp.full((8, 128), a, jnp.int32).astype(F32)
    weights = (
        jnp.max(coupling_weight(jnp.maximum(level_one - 1.0, 0.0))),
        jnp.max(coupling_weight(level_one)),
    )
    for side, buf in enumerate((below, above)):

        @pl.when(jnp.logical_not(has_al[side]))
        def _():
            def clear(n, _):
                for part in range(2):
                    buf[part, n] = jnp.zeros((GROUPS, SUB, R2), F32)
                return 0

            lax.fori_loop(0, P_SIZE, clear, 0)

    fetch_acc.wait()

    total = w_own[...]
    lower = jnp.zeros((8, 128), jnp.int32)
    for j, copy in enumerate(quad_copies):
        copy.wait_recv()
        got = w_quad[j]
        total = total + got
        lower = lower + jnp.where((q + QUAD - 1 - j) % QUAD < q, got, 0)
    w_total[...] = total
    for copy in y_copies:
        copy.start()
    for j, copy in enumerate(y_copies):
        copy.wait_recv()
        lower = lower + jnp.where((y + quads - 1 - j) % quads < y, w_ys[j], 0)
    edge = lower.astype(F32)
    tile = (P_SIZE // 8, R2 // 128)
    nodes = iota((P_SIZE, R2), 0).astype(F32) / (P_SIZE - 1)
    radius_one = radius_zero + jnp.tile(edge, tile) + jnp.tile(wide, tile) * nodes
    radius_two = radius_zero + radial_step * iota((P_SIZE, R2), 1).astype(F32)
    level_rows = jnp.full((P_SIZE, R2), a, jnp.int32).astype(F32)
    cent_one = level_rows * (level_rows + 1.0) / (2.0 * radius_one * radius_one) - 2.0 / radius_one
    potn[...] = cent_one + 1.0 / jnp.maximum(radius_one, radius_two)
    reach[...] = field[0] * radius_one / dipole_scale

    def fill_pot(n, _):
        pot[n] = cent2[...] + potn[pl.ds(n, 1)][None]
        return 0

    lax.fori_loop(0, P_SIZE, fill_pot, 0)

    def blocks_of(k, old, new):
        factor = dt_step / k

        def one(block, _):
            c, g = block // GROUPS, block % GROUPS
            xb = xbs[old, block]
            inner = dot(ke[...], xb)
            outer = dot(xb, outer_m[...])
            rest = outer + pot[:, g].reshape(ROWS, R2) * xs[old, c, :, g].reshape(ROWS, R2)
            op[0, block] = rest[0:SUB]
            op[1, block] = rest[ROWS - SUB :]
            image = (inner * scale + rest) * jnp.where(c == 1, factor, -factor)
            d = 1 - c
            image3 = image.reshape(P_SIZE, SUB, R2)
            xs[new, d, :, g] = image3
            inner_planes = slice(1, P_SIZE - 1)
            out[d, inner_planes, g] = out[d, inner_planes, g] + image3[inner_planes]
            if k < ORDER:
                target = d * GROUPS + g
                xbs[new, target] = image.astype(BF16)
                partial_sums(new, target)
            return 0

        lax.fori_loop(0, 2 * GROUPS, one, 0)

    def mix_planes(first, count):
        rows = pl.ds(first, count)
        size = count * L2

        def one(c, _):
            mixed = jnp.zeros((size, R2), F32)
            for side in range(2):
                value = bufs[side][c, rows].reshape(size, R2)
                high = value.astype(BF16)
                low = (value - high.astype(F32)).astype(BF16)
                match = mix[side, 0:size, 0:size]
                mixed = mixed + weights[side] * (dot(match, high) + dot(match, low))
            sign = jnp.where(c == 1, 1.0, -1.0)
            mixed = mixed.reshape(count, GROUPS, SUB, R2)
            far = reach[rows][:, None, None, :] * sign
            out[1 - c, rows] = out[1 - c, rows] + far * mixed
            return 0

        lax.fori_loop(0, 2, one, 0)

    def receive_planes(first, count):
        for i in range(first // CHUNK, (first + count) // CHUNK):
            for side in range(2):

                @pl.when(has_al[side])
                def _():
                    bulk_arrival(side, i).wait_recv()

        mix_planes(first, count)

    def finish_rims(k, old, new):
        factor = dt_step / k
        for side in range(2):

            @pl.when(has_row[side])
            def _():
                rim_arrival(k - 1, side).wait_recv()

        for c in range(2):
            for side in range(2):
                mine = op[side, c * GROUPS : (c + 1) * GROUPS]
                if k == 1:
                    theirs = psi_op[side][c]
                else:
                    theirs = mine
                raw = (rim_out[k - 1, side, c] + rim_in[k - 1, side, c]) + (mine + theirs)
                raw = jnp.where(has_row[side], raw, 0.0)
                xs[new, 1 - c, ends[side]] = raw * (factor if c == 1 else -factor)
        if k < ORDER:
            rim_sums(k, new)
            send_rims(k)
        for c in range(2):
            for end in ends:
                out[c, end] = out[c, end] + xs[new, c, end]
            if k < ORDER:
                for g in range(GROUPS):
                    for first, place in ((0, 0), (P_SIZE - 2, ROWS - 2 * SUB)):
                        pair = xs[new, c, first : first + 2, g].reshape(2 * SUB, R2)
                        xbs[new, c * GROUPS + g, place : place + 2 * SUB] = pair.astype(BF16)

    blocks_of(1, 0, 1)
    psi_op = []
    for side in range(2):

        @pl.when(has_row[side])
        def _():
            psi_arrival(side).wait_recv()

        parts = []
        for c in range(2):
            other = psi_rim[side, c]
            there = dot(other.reshape(L2, R2).astype(BF16), outer_m[...])
            parts.append(there.reshape(GROUPS, SUB, R2) + pot[ends[side]] * other)
        psi_op.append(parts)
    finish_rims(1, 0, 1)
    for k in range(2, ORDER + 1):
        if k < ORDER:
            start_direct(k)
        pass_on(k - 1)
        old, new = (k - 1) % 2, k % 2
        blocks_of(k, old, new)
        if k == 4:
            receive_planes(0, 8)
            receive_planes(8, 8)
        finish_rims(k, old, new)
    receive_planes(16, 8)
    receive_planes(24, 4)
    receive_planes(28, 4)

    for copy in quad_copies + y_copies:
        copy.wait_send()
    for side in range(2):

        @pl.when(has_row[side])
        def _():
            psi_copy(side).wait_send()
            for k in range(ORDER):
                rim_copy(k, side).wait_send()

        @pl.when(has_al[side])
        def _():
            for i in range(CHUNKS):
                bulk_copy(side, i).wait_send()

        @pl.when(pass_side[side])
        def _():
            for i in range(DIRECT, CHUNKS):
                pass_copy(side, i).wait_send()


def local(al_size, row_size, psi, angular, widths, field, elem_matrix, outer_matrix):
    shape = (2, P_SIZE, GROUPS, SUB, R2)
    plane = (GROUPS, SUB, R2)
    quads = row_size // QUAD
    dma = pltpu.SemaphoreType.DMA
    vmem = pl.BlockSpec(memory_space=pltpu.VMEM)
    smem = pl.BlockSpec(memory_space=pltpu.SMEM)
    hbm = pl.BlockSpec(memory_space=pltpu.HBM)
    blocks = 2 * GROUPS
    advanced = pl.pallas_call(
        functools.partial(kernel, al_size, row_size),
        out_shape=jax.ShapeDtypeStruct(shape, F32),
        in_specs=[hbm, hbm, smem, smem, hbm, hbm],
        out_specs=vmem,
        scratch_shapes=[
            pltpu.VMEM((2,) + shape, F32),
            pltpu.VMEM((2, blocks, ROWS, R2), BF16),
            pltpu.VMEM((P_SIZE,) + plane, F32),
            pltpu.VMEM(shape, F32),
            pltpu.VMEM(shape, F32),
            pltpu.VMEM((R2, R2), BF16),
            pltpu.VMEM((ROWS, ROWS), BF16),
            pltpu.VMEM((2 * SUB, ROWS), BF16),
            pltpu.VMEM((2, MIXROWS, MIXROWS), BF16),
            pltpu.VMEM(plane, F32),
            pltpu.VMEM((P_SIZE, R2), F32),
            pltpu.VMEM((P_SIZE, R2), F32),
            pltpu.VMEM((2, 2) + plane, F32),
            pltpu.VMEM((ORDER, 2, 2) + plane, F32),
            pltpu.VMEM((ORDER, 2, 2) + plane, F32),
            pltpu.VMEM((2, blocks, SUB, R2), F32),
            pltpu.VMEM((2, blocks, SUB, R2), F32),
            pltpu.VMEM((8, 128), jnp.int32),
            pltpu.VMEM((QUAD - 1, 8, 128), jnp.int32),
            pltpu.VMEM((8, 128), jnp.int32),
            pltpu.VMEM((quads - 1, 8, 128), jnp.int32),
            pltpu.VMEM((L2, L2), jnp.int32),
            pltpu.VMEM((P_SIZE, P_SIZE), BF16),
            pltpu.VMEM((CHUNKS - DIRECT, 2, CHUNK) + plane, F32),
            dma((5,)),
            dma((2, CHUNKS)),
            dma((2, CHUNKS)),
            dma((ORDER, 2)),
            dma((ORDER, 2)),
            dma((2,)),
            dma((2,)),
            dma((QUAD + quads - 2,)),
            dma((QUAD + quads - 2,)),
            dma((CHUNKS - DIRECT,)),
            dma((CHUNKS - DIRECT,)),
            pltpu.SemaphoreType.REGULAR,
            pltpu.SemaphoreType.REGULAR,
            pltpu.SemaphoreType.REGULAR,
        ],
        compiler_params=pltpu.CompilerParams(
            collective_id=0, has_side_effects=True, vmem_limit_bytes=48 * 1024 * 1024
        ),
    )(*[pltpu.with_memory_space_constraint(v, pltpu.HBM) if i in (0,1,4,5) else v for i,v in enumerate((psi.reshape(shape), angular, widths, field, elem_matrix, outer_matrix))])
    return advanced.reshape(psi.shape)


def solution(mesh):
    placed = (P("al", None, "row", None, None), P(), P("row"), P(), P(), P())
    return jax.shard_map(
        functools.partial(local, mesh.shape["al"], mesh.shape["row"]),
        mesh=mesh,
        in_specs=placed,
        out_specs=P("al", None, "row", None, None),
        check_vma=False,
    )
```

```python
import functools

import jax
import jax.numpy as jnp
from jax import lax
from jax.experimental import pallas as pl
from jax.experimental.pallas import tpu as pltpu
from jax.sharding import PartitionSpec as P

MESH = pl.DeviceIdType.MESH
F32 = jnp.float32
BF16 = jnp.bfloat16

P_SIZE = 32
L2 = 16
R2 = 512
ORDER = 4
SUB = 8
GROUPS = L2 // SUB
ROWS = P_SIZE * SUB
QUAD = 4
CHUNKS = 16
CHUNK = P_SIZE // CHUNKS
DIRECT = 8
AHEAD = (0, 2, 2, 4, 8)
PASSED = (8, 8, 10, 12, 16)
MIXPLANES = 8
MIXROWS = MIXPLANES * L2
X_SIZE = 4

dt_step = 0.35
radius_zero = 8.0
radial_step = 0.25
dipole_scale = 64.0


def iota(shape, dim):
    return lax.broadcasted_iota(jnp.int32, shape, dim)


def dot(a, b):
    return jnp.dot(a, b, preferred_element_type=F32)


def dot_lhs_t(a, b):
    return lax.dot_general(a, b, (((0,), (0,)), ((), ())), preferred_element_type=F32)


def ones_where(mask):
    return jnp.where(mask, 1.0, 0.0).astype(BF16)


def spread(size, inner, count):
    rows = iota((size, count), 0)
    rows = rows // inner if inner else rows % count
    return ones_where(rows == iota((size, count), 1))


def spread_t(size, inner, count):
    cols = iota((count, size), 1)
    cols = cols // inner if inner else cols % count
    return ones_where(cols == iota((count, size), 0))


def coupling_weight(level):
    return (level + 1.0) / jnp.sqrt((2.0 * level + 1.0) * (2.0 * level + 3.0))


def kernel(
    al_size, row_size,
    psi, ang_hbm, widths, field, elem_hbm, outer_hbm,
    out,
    xs, xbs, pot, below, above, outer_m, ke, kp, mix, cent2, potn, reach,
    psi_rim, rim_in, rim_out, op, partial, w_own, w_quad, w_total, w_ys, ang, elem, held,
    local_sem, bulk_send, bulk_recv, rim_send, rim_recv, psi_send, psi_recv, w_send, w_recv,
    held_recv, pass_send, near_sem, twice_sem, row_sem,
):
    a = lax.axis_index("al")
    r = lax.axis_index("row")
    quads = row_size // QUAD
    q = r % QUAD
    y = r // QUAD
    x = a % X_SIZE
    has_al = (a > 0, a < al_size - 1)
    wraps = (has_al[0] & (x == 0), has_al[1] & (x == X_SIZE - 1))
    at_end = (x == 0) | (x == X_SIZE - 1)
    inward = jnp.where(x == 0, 1, -1)
    passes = at_end & (a + inward * X_SIZE >= 0) & (a + inward * X_SIZE < al_size)
    pass_from = a + inward * (X_SIZE - 1)
    pass_to = a + inward * X_SIZE
    pass_side = (passes & (x == X_SIZE - 1), passes & (x == 0))
    has_row = (r > 0, r < row_size - 1)
    odd = x % 2 == 1
    even = jnp.logical_not(odd)
    al_peers = [(has_al[0], a - 1), (has_al[1], a + 1), (at_end, a + inward * (X_SIZE - 1))]

    fetch_psi = pltpu.make_async_copy(psi, xs.at[0], local_sem.at[0])
    fetch_acc = pltpu.make_async_copy(psi, out, local_sem.at[1])
    fetch_outer = pltpu.make_async_copy(outer_hbm, outer_m, local_sem.at[2])
    fetch_small = [
        pltpu.make_async_copy(elem_hbm, elem, local_sem.at[3]),
        pltpu.make_async_copy(ang_hbm, ang, local_sem.at[4]),
    ]
    for fetch in fetch_small:
        fetch.start()
    fetch_psi.start()
    fetch_outer.start()
    fetch_acc.start()

    barrier = pltpu.get_barrier_semaphore()
    quad_peers = [y * QUAD + (q + j) % QUAD for j in range(1, QUAD)]
    y_peers = [((y + j) % quads) * QUAD + q for j in range(1, quads)]

    def signal_al(sem):
        for present, peer in al_peers:

            @pl.when(present)
            def _():
                pl.semaphore_signal(sem, inc=1, device_id={"al": peer}, device_id_type=MESH)

    al_count = 0
    for present, _ in al_peers:
        al_count = al_count + present.astype(jnp.int32)
    row_count = QUAD - 1 + quads - 1
    for present in has_row:
        row_count = row_count + present.astype(jnp.int32)

    @pl.when(odd)
    def _():
        signal_al(barrier)

    w_own[...] = jnp.full((8, 128), widths[0], jnp.int32)
    ends = (0, P_SIZE - 1)

    def rim_rounded(slot, c, end):
        return xs[slot, c, ends[end]].astype(BF16).astype(F32)

    def rim_copy(k, side):
        return pltpu.make_async_remote_copy(
            src_ref=rim_out.at[k, side],
            dst_ref=rim_in.at[k, 1 - side],
            send_sem=rim_send.at[k, side],
            recv_sem=rim_recv.at[k, 1 - side],
            device_id={"row": r + 2 * side - 1},
            device_id_type=MESH,
        )

    def rim_arrival(k, side):
        return pltpu.make_async_remote_copy(
            src_ref=rim_out.at[k, 1 - side],
            dst_ref=rim_in.at[k, side],
            send_sem=rim_send.at[k, 1 - side],
            recv_sem=rim_recv.at[k, side],
            device_id={"row": r + 2 * side - 1},
            device_id_type=MESH,
        )

    def psi_copy(side):
        return pltpu.make_async_remote_copy(
            src_ref=psi.at[:, ends[side]],
            dst_ref=psi_rim.at[1 - side],
            send_sem=psi_send.at[side],
            recv_sem=psi_recv.at[1 - side],
            device_id={"row": r + 2 * side - 1},
            device_id_type=MESH,
        )

    def psi_arrival(side):
        return pltpu.make_async_remote_copy(
            src_ref=psi.at[:, ends[1 - side]],
            dst_ref=psi_rim.at[side],
            send_sem=psi_send.at[1 - side],
            recv_sem=psi_recv.at[side],
            device_id={"row": r + 2 * side - 1},
            device_id_type=MESH,
        )

    def rim_sums(k, slot):
        for c in range(2):
            low, high = rim_rounded(slot, c, 0), rim_rounded(slot, c, 1)
            for side in range(2):
                part = partial[side, c * GROUPS : (c + 1) * GROUPS]
                rim_out[k, side, c] = part + corner[side][0] * low + corner[side][1] * high

    def send_rims(k):
        for side in range(2):

            @pl.when(has_row[side])
            def _():
                rim_copy(k, side).start()

    bufs = (below, above)

    def bulk_copy(side, i):
        return pltpu.make_async_remote_copy(
            src_ref=psi.at[:, pl.ds(i * CHUNK, CHUNK)],
            dst_ref=bufs[1 - side].at[:, pl.ds(i * CHUNK, CHUNK)],
            send_sem=bulk_send.at[side, i],
            recv_sem=bulk_recv.at[1 - side, i],
            device_id={"al": a + 2 * side - 1},
            device_id_type=MESH,
        )

    def relay_copy(side, i):
        ahead = (2 * side - 1) * (1 - X_SIZE)
        return pltpu.make_async_remote_copy(
            src_ref=psi.at[:, pl.ds(i * CHUNK, CHUNK)],
            dst_ref=held.at[i - DIRECT],
            send_sem=bulk_send.at[side, i],
            recv_sem=held_recv.at[i - DIRECT],
            device_id={"al": a + ahead},
            device_id_type=MESH,
        )

    def pass_copy(side, i):
        return pltpu.make_async_remote_copy(
            src_ref=held.at[i - DIRECT],
            dst_ref=bufs[1 - side].at[:, pl.ds(i * CHUNK, CHUNK)],
            send_sem=pass_send.at[i - DIRECT],
            recv_sem=bulk_recv.at[1 - side, i],
            device_id={"al": pass_to},
            device_id_type=MESH,
        )

    def pass_on(turn):
        for i in range(PASSED[turn], PASSED[turn + 1]):

            @pl.when(passes)
            def _():
                pltpu.make_async_remote_copy(
                    src_ref=psi.at[:, pl.ds(i * CHUNK, CHUNK)],
                    dst_ref=held.at[i - DIRECT],
                    send_sem=bulk_send.at[0, i],
                    recv_sem=held_recv.at[i - DIRECT],
                    device_id={"al": pass_from},
                    device_id_type=MESH,
                ).wait_recv()

            for side in range(2):

                @pl.when(pass_side[side])
                def _():
                    pass_copy(side, i).start()

    def start_bulk():
        for i in range(CHUNKS):
            for side in range(2):

                @pl.when(has_al[side] & jnp.logical_not(wraps[side]))
                def _():
                    bulk_copy(side, i).start()

                if i >= DIRECT:

                    @pl.when(wraps[side])
                    def _():
                        relay_copy(side, i).start()

    def start_direct(turn):
        for side in range(2):

            @pl.when(wraps[side])
            def _():
                for i in range(AHEAD[turn], AHEAD[turn + 1]):
                    bulk_copy(side, i).start()

    def bulk_arrival(side, i):
        return pltpu.make_async_remote_copy(
            src_ref=psi.at[:, pl.ds(i * CHUNK, CHUNK)],
            dst_ref=bufs[side].at[:, pl.ds(i * CHUNK, CHUNK)],
            send_sem=bulk_send.at[1 - side, i],
            recv_sem=bulk_recv.at[side, i],
            device_id={"al": a + 2 * side - 1},
            device_id_type=MESH,
        )

    def width_copy(j, source, target, peer):
        return pltpu.make_async_remote_copy(
            src_ref=source,
            dst_ref=target,
            send_sem=w_send.at[j],
            recv_sem=w_recv.at[j],
            device_id={"row": peer},
            device_id_type=MESH,
        )

    quad_copies = [width_copy(j, w_own, w_quad.at[j], quad_peers[j]) for j in range(QUAD - 1)]
    y_copies = [
        width_copy(QUAD - 1 + j, w_total, w_ys.at[j], y_peers[j]) for j in range(quads - 1)
    ]

    @pl.when(even)
    def _():
        pl.semaphore_wait(barrier, al_count)
        signal_al(near_sem)

    @pl.when(odd)
    def _():
        pl.semaphore_wait(near_sem, al_count)
        signal_al(twice_sem)
        for peer in quad_peers + y_peers:
            pl.semaphore_signal(barrier, inc=1, device_id={"row": peer}, device_id_type=MESH)
        for side in range(2):

            @pl.when(has_row[side])
            def _():
                pl.semaphore_signal(
                    barrier, inc=1, device_id={"row": r + 2 * side - 1}, device_id_type=MESH
                )

    start_bulk()

    start_direct(0)

    wide = jnp.full((8, 128), widths[0], jnp.int32).astype(F32)
    scale = jnp.max(4.0 / (wide * wide))
    for fetch in fetch_small:
        fetch.wait()
    ef = elem[...].astype(F32)
    ri, ci = iota((P_SIZE, P_SIZE), 0), iota((P_SIZE, P_SIZE), 1)
    corner = [[jnp.sum(jnp.where((ri == i) & (ci == k), ef, 0.0)) * scale for k in ends] for i in ends]
    wide_rows = dot(spread(ROWS, SUB, P_SIZE), elem[...]).astype(BF16)
    kron = dot(wide_rows, spread_t(ROWS, SUB, P_SIZE))
    kr, kc = iota((ROWS, ROWS), 0), iota((ROWS, ROWS), 1)
    kron = jnp.where(kr % SUB == kc % SUB, kron, 0.0)
    ke[...] = kron.astype(BF16)
    inside = (kc >= SUB) & (kc < ROWS - SUB)
    kron = jnp.where(inside, kron, 0.0)
    kp[...] = jnp.concatenate([kron[0:SUB], kron[ROWS - SUB :]], 0).astype(BF16)

    fetch_psi.wait()
    fetch_outer.wait()

    def partial_sums(slot, block):
        sums = dot(kp[...], xbs[slot, block]) * scale
        partial[0, block] = sums[0:SUB]
        partial[1, block] = sums[SUB:]

    def round_start(block, _):
        c, g = block // GROUPS, block % GROUPS
        xbs[0, block] = xs[0, c, :, g].reshape(ROWS, R2).astype(BF16)
        partial_sums(0, block)
        return 0

    lax.fori_loop(0, 2 * GROUPS, round_start, 0)

    rim_sums(0, 0)

    @pl.when(odd)
    def _():
        pl.semaphore_wait(barrier, row_count)
        pl.semaphore_signal(row_sem, inc=1, device_id={"al": a - 1}, device_id_type=MESH)

    @pl.when(even)
    def _():
        pl.semaphore_wait(row_sem, 1)

    for copy in quad_copies:
        copy.start()
    for side in range(2):

        @pl.when(has_row[side])
        def _():
            psi_copy(side).start()

    send_rims(0)
    start_direct(1)

    @pl.when(even)
    def _():
        pl.semaphore_wait(twice_sem, al_count)

    pass_on(0)
    angf = ang[...]
    slots = iota((L2, L2), 0)

    def one_hot(level):
        row = jnp.sum(jnp.where(slots == level, angf, 0), axis=0, keepdims=True)
        return ones_where(jnp.broadcast_to(row, (L2, L2)) == slots)

    own_hot = one_hot(a)
    mr, mc = iota((MIXROWS, MIXROWS), 0), iota((MIXROWS, MIXROWS), 1)
    for side in range(2):
        level = jnp.clip(a + 2 * side - 1, 0, al_size - 1)
        match = dot_lhs_t(own_hot, one_hot(level)).astype(BF16)
        tall = dot(spread(MIXROWS, 0, L2), match).astype(BF16)
        full = dot(tall, spread_t(MIXROWS, 0, L2))
        mix[side] = jnp.where(mr // L2 == mc // L2, full, 0.0).astype(BF16)
    momenta = iota((L2, R2), 0)
    square = dot_lhs_t(own_hot, (momenta * (momenta + 1)).astype(F32).astype(BF16))
    radius_two = radius_zero + radial_step * iota((L2, R2), 1).astype(F32)
    cent = square / (2.0 * radius_two * radius_two) - 2.0 / radius_two
    cent2[...] = cent.reshape(GROUPS, SUB, R2)

    level_one = jnp.full((8, 128), a, jnp.int32).astype(F32)
    weights = (
        jnp.max(coupling_weight(jnp.maximum(level_one - 1.0, 0.0))),
        jnp.max(coupling_weight(level_one)),
    )
    for side, buf in enumerate((below, above)):

        @pl.when(jnp.logical_not(has_al[side]))
        def _():
            def clear(n, _):
                for part in range(2):
                    buf[part, n] = jnp.zeros((GROUPS, SUB, R2), F32)
                return 0

            lax.fori_loop(0, P_SIZE, clear, 0)

    fetch_acc.wait()

    total = w_own[...]
    lower = jnp.zeros((8, 128), jnp.int32)
    for j, copy in enumerate(quad_copies):
        copy.wait_recv()
        got = w_quad[j]
        total = total + got
        lower = lower + jnp.where((q + QUAD - 1 - j) % QUAD < q, got, 0)
    w_total[...] = total
    for copy in y_copies:
        copy.start()
    for j, copy in enumerate(y_copies):
        copy.wait_recv()
        lower = lower + jnp.where((y + quads - 1 - j) % quads < y, w_ys[j], 0)
    edge = lower.astype(F32)
    tile = (P_SIZE // 8, R2 // 128)
    nodes = iota((P_SIZE, R2), 0).astype(F32) / (P_SIZE - 1)
    radius_one = radius_zero + jnp.tile(edge, tile) + jnp.tile(wide, tile) * nodes
    radius_two = radius_zero + radial_step * iota((P_SIZE, R2), 1).astype(F32)
    level_rows = jnp.full((P_SIZE, R2), a, jnp.int32).astype(F32)
    cent_one = level_rows * (level_rows + 1.0) / (2.0 * radius_one * radius_one) - 2.0 / radius_one
    potn[...] = cent_one + 1.0 / jnp.maximum(radius_one, radius_two)
    reach[...] = field[0] * radius_one / dipole_scale

    def fill_pot(n, _):
        pot[n] = cent2[...] + potn[pl.ds(n, 1)][None]
        return 0

    lax.fori_loop(0, P_SIZE, fill_pot, 0)

    def blocks_of(k, old, new):
        factor = dt_step / k

        def one(block, _):
            c, g = block // GROUPS, block % GROUPS
            xb = xbs[old, block]
            inner = dot(ke[...], xb)
            outer = dot(xb, outer_m[...])
            rest = outer + pot[:, g].reshape(ROWS, R2) * xs[old, c, :, g].reshape(ROWS, R2)
            op[0, block] = rest[0:SUB]
            op[1, block] = rest[ROWS - SUB :]
            image = (inner * scale + rest) * jnp.where(c == 1, factor, -factor)
            d = 1 - c
            image3 = image.reshape(P_SIZE, SUB, R2)
            xs[new, d, :, g] = image3
            inner_planes = slice(1, P_SIZE - 1)
            out[d, inner_planes, g] = out[d, inner_planes, g] + image3[inner_planes]
            if k < ORDER:
                target = d * GROUPS + g
                xbs[new, target] = image.astype(BF16)
                partial_sums(new, target)
            return 0

        lax.fori_loop(0, 2 * GROUPS, one, 0)

    def mix_planes(first, count):
        rows = pl.ds(first, count)
        size = count * L2

        def one(c, _):
            mixed = jnp.zeros((size, R2), F32)
            for side in range(2):
                value = bufs[side][c, rows].reshape(size, R2)
                high = value.astype(BF16)
                low = (value - high.astype(F32)).astype(BF16)
                match = mix[side, 0:size, 0:size]
                mixed = mixed + weights[side] * (dot(match, high) + dot(match, low))
            sign = jnp.where(c == 1, 1.0, -1.0)
            mixed = mixed.reshape(count, GROUPS, SUB, R2)
            far = reach[rows][:, None, None, :] * sign
            out[1 - c, rows] = out[1 - c, rows] + far * mixed
            return 0

        lax.fori_loop(0, 2, one, 0)

    def receive_planes(first, count):
        for i in range(first // CHUNK, (first + count) // CHUNK):
            for side in range(2):

                @pl.when(has_al[side])
                def _():
                    bulk_arrival(side, i).wait_recv()

        mix_planes(first, count)

    def finish_rims(k, old, new):
        factor = dt_step / k
        for side in range(2):

            @pl.when(has_row[side])
            def _():
                rim_arrival(k - 1, side).wait_recv()

        for c in range(2):
            for side in range(2):
                mine = op[side, c * GROUPS : (c + 1) * GROUPS]
                if k == 1:
                    theirs = psi_op[side][c]
                else:
                    theirs = mine
                raw = (rim_out[k - 1, side, c] + rim_in[k - 1, side, c]) + (mine + theirs)
                raw = jnp.where(has_row[side], raw, 0.0)
                xs[new, 1 - c, ends[side]] = raw * (factor if c == 1 else -factor)
        if k < ORDER:
            rim_sums(k, new)
            send_rims(k)
        for c in range(2):
            for end in ends:
                out[c, end] = out[c, end] + xs[new, c, end]
            if k < ORDER:
                for g in range(GROUPS):
                    for first, place in ((0, 0), (P_SIZE - 2, ROWS - 2 * SUB)):
                        pair = xs[new, c, first : first + 2, g].reshape(2 * SUB, R2)
                        xbs[new, c * GROUPS + g, place : place + 2 * SUB] = pair.astype(BF16)

    blocks_of(1, 0, 1)
    psi_op = []
    for side in range(2):

        @pl.when(has_row[side])
        def _():
            psi_arrival(side).wait_recv()

        parts = []
        for c in range(2):
            other = psi_rim[side, c]
            there = dot(other.reshape(L2, R2).astype(BF16), outer_m[...])
            parts.append(there.reshape(GROUPS, SUB, R2) + pot[ends[side]] * other)
        psi_op.append(parts)
    finish_rims(1, 0, 1)
    for k in range(2, ORDER + 1):
        if k < ORDER:
            start_direct(k)
        pass_on(k - 1)
        old, new = (k - 1) % 2, k % 2
        blocks_of(k, old, new)
        if k == 4:
            receive_planes(0, 8)
            receive_planes(8, 8)
        finish_rims(k, old, new)
    receive_planes(16, 8)
    receive_planes(24, 4)
    receive_planes(28, 4)

    for copy in quad_copies + y_copies:
        copy.wait_send()
    for side in range(2):

        @pl.when(has_row[side])
        def _():
            psi_copy(side).wait_send()
            for k in range(ORDER):
                rim_copy(k, side).wait_send()

        @pl.when(has_al[side])
        def _():
            for i in range(CHUNKS):
                bulk_copy(side, i).wait_send()

        @pl.when(pass_side[side])
        def _():
            for i in range(DIRECT, CHUNKS):
                pass_copy(side, i).wait_send()


def local(al_size, row_size, psi, angular, widths, field, elem_matrix, outer_matrix):
    shape = (2, P_SIZE, GROUPS, SUB, R2)
    plane = (GROUPS, SUB, R2)
    quads = row_size // QUAD
    dma = pltpu.SemaphoreType.DMA
    vmem = pl.BlockSpec(memory_space=pltpu.VMEM)
    smem = pl.BlockSpec(memory_space=pltpu.SMEM)
    hbm = pl.BlockSpec(memory_space=pltpu.HBM)
    blocks = 2 * GROUPS
    advanced = pl.pallas_call(
        functools.partial(kernel, al_size, row_size),
        out_shape=jax.ShapeDtypeStruct(shape, F32),
        in_specs=[hbm, hbm, smem, smem, hbm, hbm],
        out_specs=vmem,
        scratch_shapes=[
            pltpu.VMEM((2,) + shape, F32),
            pltpu.VMEM((2, blocks, ROWS, R2), BF16),
            pltpu.VMEM((P_SIZE,) + plane, F32),
            pltpu.VMEM(shape, F32),
            pltpu.VMEM(shape, F32),
            pltpu.VMEM((R2, R2), BF16),
            pltpu.VMEM((ROWS, ROWS), BF16),
            pltpu.VMEM((2 * SUB, ROWS), BF16),
            pltpu.VMEM((2, MIXROWS, MIXROWS), BF16),
            pltpu.VMEM(plane, F32),
            pltpu.VMEM((P_SIZE, R2), F32),
            pltpu.VMEM((P_SIZE, R2), F32),
            pltpu.VMEM((2, 2) + plane, F32),
            pltpu.VMEM((ORDER, 2, 2) + plane, F32),
            pltpu.VMEM((ORDER, 2, 2) + plane, F32),
            pltpu.VMEM((2, blocks, SUB, R2), F32),
            pltpu.VMEM((2, blocks, SUB, R2), F32),
            pltpu.VMEM((8, 128), jnp.int32),
            pltpu.VMEM((QUAD - 1, 8, 128), jnp.int32),
            pltpu.VMEM((8, 128), jnp.int32),
            pltpu.VMEM((quads - 1, 8, 128), jnp.int32),
            pltpu.VMEM((L2, L2), jnp.int32),
            pltpu.VMEM((P_SIZE, P_SIZE), BF16),
            pltpu.VMEM((CHUNKS - DIRECT, 2, CHUNK) + plane, F32),
            dma((5,)),
            dma((2, CHUNKS)),
            dma((2, CHUNKS)),
            dma((ORDER, 2)),
            dma((ORDER, 2)),
            dma((2,)),
            dma((2,)),
            dma((QUAD + quads - 2,)),
            dma((QUAD + quads - 2,)),
            dma((CHUNKS - DIRECT,)),
            dma((CHUNKS - DIRECT,)),
            pltpu.SemaphoreType.REGULAR,
            pltpu.SemaphoreType.REGULAR,
            pltpu.SemaphoreType.REGULAR,
        ],
        compiler_params=pltpu.CompilerParams(
            collective_id=0, has_side_effects=True, vmem_limit_bytes=48 * 1024 * 1024
        ),
    )(*[pltpu.with_memory_space_constraint(v, pltpu.HBM) if i in (0,1,4,5) else v for i,v in enumerate((psi.reshape(shape), angular, widths, field, elem_matrix, outer_matrix))])
    return advanced.reshape(psi.shape)


def solution(mesh):
    placed = (P("al", None, "row", None, None), P(), P("row"), P(), P(), P())
    return jax.shard_map(
        functools.partial(local, mesh.shape["al"], mesh.shape["row"]),
        mesh=mesh,
        in_specs=placed,
        out_specs=P("al", None, "row", None, None),
        check_vma=False,
    )
```
